128 devices in a mesh: rows: 16 (over x, y), cols: 8 (over z, core).
Axes of the slice: x: 4, y: 4, z: 4, core: 2. Of those that a mesh axis runs over, the one named last changes fastest.
Arguments:
- affinity: bfloat16 [8, 128, 8, 8, 4096], P(None, 'rows', 'cols'), may hold values from -6 to 6
- block_columns: int32 [8, 128, 8, 8], P(None, 'rows', 'cols'), may hold values from 0 to 127
- block_counts: int32 [8, 128, 8], P(None, 'rows', 'cols'), may hold values from 0 to 8
- inv_degree: float32 [8, 128, 64], P('cols', 'rows'), may hold values from 0.4 to 6.1
- panel: float32 [8, 128, 4096], P('cols', 'rows'), may hold values from -6 to 6
Outputs:
- panel_out: float32 [8, 128, 4096], P('cols', 'rows')
The draws below stay inside these ranges and needn't reach their ends.
Inputs may be any that keep to these rules, and one draw needn't show every extreme that they name: `block_columns`: slots at or past a block row's count are ignored; listed block columns may repeat, and their blocks then add.
All inputs are finite; a program needn't handle non-finite values.
Results may differ from the reference program's by a relative error of at most 0.019.
Values may be sent and summed in bfloat16 or wider, within the bound.
A program may use at most 128 MiB of HBM per device.

```python
import jax
import jax.numpy as jnp
from jax import lax

B = 64
K = 64
MAXB = 8
ITERS = 2
NBR = 1024
N = 65536
N_COLS = 8


def draw_block_counts(key, part):
    shape = (N_COLS, NBR // N_COLS, N_COLS)
    first, second, third = jax.random.split(jax.random.fold_in(key, 7), 3)
    base = jax.random.randint(first, shape, 0, MAXB // 2 + 1)
    heavy = jax.random.randint(second, shape, 0, 4) == 0
    upper = MAXB - jax.random.randint(third, shape, 0, 2)
    counts = jnp.where(heavy, upper, base).astype(jnp.int32)
    counts = counts.at[0, 0, 0].set(MAXB)
    counts = counts.at[0, 0, N_COLS - 1].set(0)
    return counts


def draw_inv_degree(key, part):
    shape = (N_COLS, NBR // N_COLS, B)
    order = lax.broadcasted_iota(jnp.float32, shape, 0) * float(NBR // N_COLS) + lax.broadcasted_iota(jnp.float32, shape, 1)
    trend = 1.0 + 2.0 * order / float(NBR)
    inner = jax.random.fold_in(key, 11)
    rough = jnp.exp(jax.random.uniform(inner, shape, jnp.float32, -0.7, 0.7))
    return rough * trend


def with_ends(result, key, low, top_value):
    extent = result.shape
    index_at = [jax.random.randint(jax.random.fold_in(key, axis), (), 0, extent[axis]) for axis in range(len(extent))]
    result = result.at[tuple(index_at)].set(low)
    longest = extent.index(max(extent))
    index_at[longest] = (index_at[longest] + 1) % extent[longest]
    return result.at[tuple(index_at)].set(top_value)


def levels(stream_key, extent, cuts, least, largest):
    def one(position, blocks):
        heights = jax.random.uniform(jax.random.fold_in(jax.random.fold_in(stream_key, 6), position), (blocks,), jnp.float32, least / len(cuts), largest / len(cuts))
        return jnp.repeat(jnp.exp(heights), extent[position] // blocks).reshape((-1,) + (1,) * (len(extent) - position - 1))

    gain = one(*cuts[0])
    for cut in cuts[1:]:
        gain = gain * one(*cut)
    return gain


def bell_draw(rng, shape, spread, bound, cuts=(), kind=jnp.bfloat16):
    entries = spread * jax.random.normal(rng, shape, jnp.float32)
    if cuts:
        entries = entries * levels(rng, shape, cuts, -0.22, 0.18)
    return jnp.clip(entries, -bound, bound).astype(kind)


def setup_inputs(seed: int = 0) -> dict:
    key_of = jax.random.split(jax.random.key(seed), 6)
    return {
        "affinity": bell_draw(key_of[0], (N_COLS, NBR // N_COLS, N_COLS, MAXB, B * B), 1.0, 6.0, ((1, 16), (2, 8))),
        "block_columns": with_ends(jax.random.randint(key_of[1], (N_COLS, NBR // N_COLS, N_COLS, MAXB), 0, NBR // N_COLS), jax.random.fold_in(key_of[1], 1), 0, (NBR // N_COLS) - 1).astype(jnp.int32),
        "block_counts": draw_block_counts(jax.random.fold_in(key_of[5], 71), 0),
        "inv_degree": draw_inv_degree(jax.random.fold_in(key_of[5], 71), 0),
        "panel": bell_draw(key_of[4], (N_COLS, NBR // N_COLS, B * K), 1.0, 6.0, ((0, 8), (1, 16)), jnp.float32),
    }


def block_terms(values_slice, columns_slice, counts_slice, panel_blocks):
    groups = values_slice.shape[0]
    block_rows = values_slice.shape[1]
    accum = jnp.zeros((groups, block_rows, B, K), jnp.float32)
    for slot_index in range(MAXB):
        picked = jnp.take(panel_blocks, columns_slice[:, :, slot_index].astype(jnp.int32), axis=0)
        live = (counts_slice > slot_index)[:, :, None, None]
        picked = jnp.where(live, picked, jnp.zeros_like(picked))
        matrix = values_slice[:, :, slot_index].reshape(groups, block_rows, B, B)
        accum = accum + jnp.einsum('giab,gibk->giak', matrix.astype(jnp.float32), picked.astype(jnp.float32))
    return accum

def reference(affinity, block_columns, block_counts, inv_degree, panel):
    per_range = NBR // N_COLS
    current = panel
    identity = jnp.eye(K, dtype=jnp.float32)
    for iteration in range(ITERS):
        scaled = (current.reshape(N_COLS, per_range, B, K) * inv_degree[..., None]).astype(jnp.bfloat16)

        def one_range(range_index, accum):
            values_slice = lax.dynamic_index_in_dim(affinity, range_index, 2, keepdims=False)
            columns_slice = lax.dynamic_index_in_dim(block_columns, range_index, 2, keepdims=False)
            counts_slice = lax.dynamic_index_in_dim(block_counts, range_index, 2, keepdims=False)
            panel_blocks = lax.dynamic_index_in_dim(scaled, range_index, 0, keepdims=False)
            term = block_terms(values_slice, columns_slice, counts_slice, panel_blocks)
            rounded = lax.optimization_barrier(term.astype(jnp.bfloat16))
            return accum + rounded.astype(jnp.float32)
        summed = lax.fori_loop(0, N_COLS, one_range, jnp.zeros((N_COLS, per_range, B, K), jnp.float32))
        rows_out = (summed * inv_degree[..., None]).reshape(-1, K)
        gram_matrix = jnp.dot(rows_out.T, rows_out, precision=lax.Precision.HIGHEST) / float(N)
        lower_factor = jnp.linalg.cholesky(gram_matrix)
        inverse = lax.linalg.triangular_solve(lower_factor, identity, left_side=True, lower=True)
        current = jnp.dot(rows_out, inverse.T, precision=lax.Precision.HIGHEST).reshape(N_COLS, per_range, B * K)
    return current
```

```python
import functools

import jax
import jax.numpy as jnp
from jax import lax
from jax.experimental import pallas as pl
from jax.experimental.pallas import tpu as pltpu
from jax.sharding import PartitionSpec as P

ITERS = 2
SIDE = 4
B = 64
G = 8
R = 8
S = 8
H = B // 2
LANES = 128
NB = 128
MESH = pl.DeviceIdType.MESH
HIGHEST = lax.Precision.HIGHEST
F32 = jnp.float32
BF16 = jnp.bfloat16


def low_lanes(rows):
    return lax.broadcasted_iota(jnp.int32, (rows, LANES), 1) < B


def trade(u, v, low):
    crossed = pltpu.roll(jnp.where(low, v, u), B, 1)
    return jnp.where(low, u, crossed), jnp.where(low, crossed, v)


def inverse_factor(gram):
    row = lax.broadcasted_iota(jnp.int32, (B, LANES), 0)
    lane = lax.broadcasted_iota(jnp.int32, (B, LANES), 1)
    m = jnp.where(lane < B, gram, jnp.where(lane - B == row, 1.0, 0.0).astype(F32))
    done = []
    for block in range(B // 8):
        height = B - 8 * block
        rows = lax.broadcasted_iota(jnp.int32, (height, LANES), 0)
        columns = [
            jnp.broadcast_to(m[:, 8 * block + j : 8 * block + j + 1], (height, LANES))
            for j in range(8)
        ]
        for j in range(8):
            ratio = columns[j] * (1.0 / columns[j][j : j + 1, :])
            ratio = jnp.where(rows > j, ratio, 0.0)
            for later in range(j + 1, 8):
                columns[later] = columns[later] - ratio * columns[later][j : j + 1, :]
            m = m - ratio * m[j : j + 1, :]
        done.append(m[:8])
        m = m[8:]
    m = jnp.concatenate(done, axis=0)
    pivots = jnp.sum(jnp.where(lane == row, m, 0.0), axis=1, keepdims=True)
    return m * lax.rsqrt(pivots)


def twice(inverse):
    low = low_lanes(B)
    upper = jnp.where(low, pltpu.roll(inverse, B, 1), 0.0)
    lower = jnp.where(low, 0.0, inverse)
    return jnp.concatenate([upper, lower], axis=0)


def times_transpose(rows, factor):
    return lax.dot_general(
        rows, factor, (((1,), (1,)), ((), ())), precision=HIGHEST, preferred_element_type=F32
    )


def kernel(
    total_rows,
    columns_ref, counts_ref, affinity_ref, inverse_ref, panel_ref,
    out_ref,
    raw, blocks, stage, degree, rows_ref, pack, gathered, table, outgoing, incoming,
    gram_z, gram_x, gram_y,
    raw_sem, ag_send, ag_recv, rs_send, rs_recv, gz_send, gz_recv, gx_send, gx_recv, gy_send, gy_recv,
):
    mine_r, mine_c = lax.axis_index("rows"), lax.axis_index("cols")
    x, y = mine_r // SIDE, lax.rem(mine_r, SIDE)
    z, core = mine_c // 2, lax.rem(mine_c, 2)

    def row_of(dx, dy):
        return lax.rem(x + dx + SIDE, SIDE) * SIDE + lax.rem(y + dy + SIDE, SIDE)

    def col_of(dz, dc):
        return lax.rem(z + dz, SIDE) * 2 + lax.rem(core + dc, 2)

    x_peers = [row_of(d, 0) for d in (1, 2, 3)]
    y_peers = [row_of(0, d) for d in (1, 2, 3)]
    order = [(2, 0), (2, 1), (1, 0), (3, 0), (1, 1), (3, 1), (0, 1)]
    z_peers = [col_of(*d) for d in order]

    for g in range(G):
        pltpu.make_async_copy(affinity_ref.at[g], raw.at[g], raw_sem.at[g]).start()

    barrier = pltpu.get_barrier_semaphore()
    for peer in x_peers + y_peers:
        pl.semaphore_signal(barrier, inc=1, device_id={"rows": peer}, device_id_type=MESH)
    for peer in z_peers:
        pl.semaphore_signal(barrier, inc=1, device_id={"cols": peer}, device_id_type=MESH)

    spread = lax.broadcasted_iota(jnp.int32, (H, B), 1) // 2 == lax.broadcasted_iota(jnp.int32, (H, B), 0)
    picked = jnp.concatenate(
        [jnp.where(spread, jnp.broadcast_to(inverse_ref[i : i + 1, :], (H, B)), 0.0) for i in range(R)], axis=0
    )
    halves = (
        lax.rem(lax.broadcasted_iota(jnp.int32, (B, LANES), 0), 2)
        == lax.broadcasted_iota(jnp.int32, (B, LANES), 1) // B
    )
    degree[...] = jnp.dot(
        picked, jnp.where(halves, 1.0, 0.0).astype(F32), precision=HIGHEST, preferred_element_type=F32
    )
    for t in range(H):
        rows_ref[pl.ds(t, R, stride=H), :] = panel_ref[:, t * LANES : (t + 1) * LANES]

    low_h = low_lanes(H)
    low_b = low_lanes(B)

    def fill_own(it):
        for pair in range(4):
            rows = slice(2 * pair * H, 2 * pair * H + B)
            scaled = rows_ref[rows, :] * degree[rows, :]
            even, odd = trade(scaled[:H], scaled[H:], low_h)
            pack[pl.ds(pair * B, H, stride=2), :] = even
            pack[pl.ds(pair * B + 1, H, stride=2), :] = odd
            gathered[it, mine_r * 4 + pair] = pack[pair * B : (pair + 1) * B, :].astype(BF16)

    def ag_copy(it, slot, number, peer):
        return pltpu.make_async_remote_copy(
            src_ref=gathered.at[it, slot],
            dst_ref=gathered.at[it, slot],
            send_sem=ag_send.at[it, number],
            recv_sem=ag_recv.at[it, slot],
            device_id={"rows": peer},
            device_id_type=MESH,
        )

    pending = []

    def expand(it, slot):
        pair = gathered[it, slot]
        zero = jnp.zeros_like(pair)
        table[2 * slot] = jnp.where(low_b, pair, zero)
        table[2 * slot + 1] = jnp.where(low_b, zero, pair)

    def all_gather(it, meanwhile):
        sent = [0]
        px, nx, py, ny = row_of(1, 0), row_of(-1, 0), row_of(0, 1), row_of(0, -1)

        def slot_of(dx, dy, pair):
            return row_of(dx, dy) * 4 + pair

        def send(dx, dy, pair, peer):
            copy = ag_copy(it, slot_of(dx, dy, pair), sent[0], peer)
            sent[0] += 1
            copy.start()
            pending.append(copy)

        def take(dx, dy, pair, *peers):
            slot = slot_of(dx, dy, pair)
            ag_copy(it, slot, 0, mine_r).wait_recv()
            for peer in peers:
                send(dx, dy, pair, peer)
            expand(it, slot)

        for peers_a, peers_b in (((px, nx), (py, ny)), ((py, ny), (px, nx))):
            for number in range(2):
                for peer_a, peer_b in zip(peers_a, peers_b):
                    send(0, 0, number, peer_a)
                    send(0, 0, 2 + number, peer_b)
        for pair in range(4):
            expand(it, slot_of(0, 0, pair))
        meanwhile(0)
        take(-1, 0, 0, px, py, ny)
        take(1, 0, 1, nx, py, ny)
        take(0, -1, 2, py, px, nx)
        take(0, 1, 3, ny, px, nx)
        take(-1, 0, 1, py, ny)
        take(1, 0, 0, py, ny)
        take(0, -1, 3, px, nx)
        take(0, 1, 2, px, nx)
        meanwhile(1)
        take(0, -1, 0, py)
        take(0, 1, 1, ny)
        take(-1, 0, 2, px)
        take(1, 0, 3, nx)
        meanwhile(2)
        take(2, 0, 0, py, ny)
        take(2, 0, 1, py, ny)
        take(0, 2, 2, px, nx)
        take(0, 2, 3, px, nx)
        meanwhile(3)
        for d in (-1, 1):
            take(d, -1, 0, py)
            take(d, 1, 1, ny)
            take(-1, d, 2, px)
            take(1, d, 3, nx)
        meanwhile(4)
        take(2, -1, 0, py)
        take(2, 1, 1, ny)
        take(-1, 2, 2, px)
        take(1, 2, 3, nx)
        meanwhile(5)
        for d in (0, -1, 1, 2):
            if d == 0:
                take(0, -1, 1)
                take(0, 1, 0)
                take(-1, 0, 3)
                take(1, 0, 2)
            else:
                take(d, -1, 1)
                take(d, 1, 0)
                take(-1, d, 3)
                take(1, d, 2)
            take(d, 2, 0)
            take(d, 2, 1)
            take(2, d, 2)
            take(2, d, 3)

    def arrange(g):
        pltpu.make_async_copy(affinity_ref.at[g], raw.at[g], raw_sem.at[g]).wait()

        def one(i, carry):
            for t in range(H):
                stage[pl.ds(t, S, stride=H), :] = raw[g, i, :, t * LANES : (t + 1) * LANES].astype(F32)
            for u in range(S // 2):
                upper, lower = trade(
                    stage[2 * u * H : (2 * u + 1) * H, :], stage[(2 * u + 1) * H : (2 * u + 2) * H, :], low_h
                )
                blocks[g * R + i, 0:H, u * LANES : (u + 1) * LANES] = upper.astype(BF16)
                blocks[g * R + i, H:B, u * LANES : (u + 1) * LANES] = lower.astype(BF16)
            return carry

        lax.fori_loop(0, R, one, 0)

    def product(g, i):
        count = counts_ref[g, i]
        right = []
        for s in range(S):
            column = jnp.where(s < count, columns_ref[g, i, s], NB)
            right.append(table[column])
        o = jnp.dot(blocks[g * R + i], jnp.concatenate(right, axis=0), preferred_element_type=F32)
        even, odd = o[:H], o[H:]
        return jnp.where(low_h, even, odd) + pltpu.roll(jnp.where(low_h, odd, even), B, 1)

    def rs_copy(it, k, peer):
        return pltpu.make_async_remote_copy(
            src_ref=outgoing.at[it, k],
            dst_ref=incoming.at[it, mine_c],
            send_sem=rs_send.at[it, k],
            recv_sem=rs_recv.at[it, mine_c],
            device_id={"cols": peer},
            device_id_type=MESH,
        )

    UNROLL = 4

    def multiply(it):
        for k, peer in enumerate(z_peers + [mine_c]):
            def some(step, carry):
                for j in range(UNROLL):
                    i = step * UNROLL + j
                    term = product(peer, i).astype(BF16)
                    at = pl.ds(pl.multiple_of(i * H, H), H)
                    if k < G - 1:
                        outgoing[it, k, at, :] = term
                    else:
                        incoming[it, mine_c, at, :] = term
                return carry

            lax.fori_loop(0, R // UNROLL, some, 0)
            if k < G - 1:
                copy = rs_copy(it, k, peer)
                copy.start()
                pending.append(copy)

    def collect(it):
        for peer in reversed(z_peers):
            pltpu.make_async_remote_copy(
                src_ref=outgoing.at[it, 0],
                dst_ref=incoming.at[it, peer],
                send_sem=rs_send.at[it, 0],
                recv_sem=rs_recv.at[it, peer],
                device_id={"cols": peer},
                device_id_type=MESH,
            ).wait_recv()
        summed = incoming[it, 0].astype(F32)
        for c in range(1, G):
            summed = summed + incoming[it, c].astype(F32)
        return summed * degree[...]

    def exchange(it, buffer, send_sem, recv_sem, at, axis, peers, slots):
        def copy(n, slot):
            return pltpu.make_async_remote_copy(
                src_ref=buffer.at[it, at],
                dst_ref=buffer.at[it, slot],
                send_sem=send_sem.at[it, n],
                recv_sem=recv_sem.at[it, slot],
                device_id={axis: peers[n]},
                device_id_type=MESH,
            )

        def start():
            for n in range(len(peers)):
                c = copy(n, at)
                c.start()
                pending.append(c)

        def finish():
            for n in range(len(peers)):
                copy(n, slots[n]).wait_recv()
            total = buffer[it, 0]
            for n in range(1, len(peers) + 1):
                total = total + buffer[it, n]
            return total

        return start, finish

    def gram_of(it):
        along_z = exchange(it, gram_z, gz_send, gz_recv, mine_c, "cols", z_peers, z_peers)
        along_x = exchange(it, gram_x, gx_send, gx_recv, x, "rows", x_peers, [p // SIDE for p in x_peers])
        along_y = exchange(it, gram_y, gy_send, gy_recv, y, "rows", y_peers, [lax.rem(p, SIDE) for p in y_peers])

        def first():
            rows = rows_ref[...]
            both = lax.dot_general(
                rows, rows, (((0,), (0,)), ((), ())), precision=HIGHEST, preferred_element_type=F32
            )
            gram = both[:B] + pltpu.roll(both[B:], B, 1)
            gram_z[it, mine_c] = jnp.where(low_h, gram[:H], pltpu.roll(gram[H:], B, 1))
            along_z[0]()

        def second():
            gram_x[it, x] = along_z[1]()
            along_x[0]()

        def third():
            gram_y[it, y] = along_x[1]()
            along_y[0]()

        def last():
            total = along_y[1]() * (1.0 / total_rows)
            return jnp.concatenate([total, pltpu.roll(total, B, 1)], axis=0)

        return first, second, third, last

    fill_own(0)
    table[NB] = jnp.zeros((B, LANES), BF16)
    pl.semaphore_wait(barrier, len(x_peers) + len(y_peers) + len(z_peers))

    shares = [(0, 1), (2,), (3,), (4, 5), (6,), (7,)]

    def arranging(n):
        for g in shares[n]:
            arrange(g)

    all_gather(0, arranging)
    multiply(0)
    rows_ref[...] = collect(0)

    first, second, third, last = gram_of(0)
    fill_own(1)

    def reducing(n):
        if n == 0:
            first()
        elif n == 3:
            second()
        elif n == 5:
            third()

    all_gather(1, reducing)
    multiply(1)
    factor = twice(inverse_factor(last()))
    rows_ref[...] = times_transpose(collect(1), factor)

    first, second, third, last = gram_of(1)
    first()
    second()
    third()
    factor = twice(inverse_factor(last()))
    rows_ref[...] = times_transpose(rows_ref[...], factor)
    for t in range(H):
        out_ref[:, t * LANES : (t + 1) * LANES] = rows_ref[pl.ds(t, R, stride=H), :]
    for copy in pending:
        copy.wait_send()


def body(affinity, block_columns, block_counts, inv_degree, panel):
    total_rows = float(affinity.shape[0] * affinity.shape[1] * lax.axis_size("rows") * B)
    dma = pltpu.SemaphoreType.DMA
    out = pl.pallas_call(
        functools.partial(kernel, total_rows),
        out_shape=jax.ShapeDtypeStruct((R, H * LANES), F32),
        in_specs=[
            pl.BlockSpec(memory_space=pltpu.SMEM),
            pl.BlockSpec(memory_space=pltpu.SMEM),
            pl.BlockSpec(memory_space=pl.ANY),
            pl.BlockSpec(memory_space=pltpu.VMEM),
            pl.BlockSpec(memory_space=pltpu.VMEM),
        ],
        out_specs=pl.BlockSpec(memory_space=pltpu.VMEM),
        scratch_shapes=[
            pltpu.VMEM((G, R, S, H * LANES), BF16),
            pltpu.VMEM((G * R, B, S * B), BF16),
            pltpu.VMEM((S * H, LANES), F32),
            pltpu.VMEM((R * H, LANES), F32),
            pltpu.VMEM((R * H, LANES), F32),
            pltpu.VMEM((R * H, LANES), F32),
            pltpu.VMEM((ITERS, NB // 2, B, LANES), BF16),
            pltpu.VMEM((NB + 1, B, LANES), BF16),
            pltpu.VMEM((ITERS, G - 1, R * H, LANES), BF16),
            pltpu.VMEM((ITERS, G, R * H, LANES), BF16),
            pltpu.VMEM((ITERS, G, H, LANES), F32),
            pltpu.VMEM((ITERS, SIDE, H, LANES), F32),
            pltpu.VMEM((ITERS, SIDE, H, LANES), F32),
            dma((G,)),
            dma((ITERS, 60)),
            dma((ITERS, NB // 2)),
            dma((ITERS, G - 1)),
            dma((ITERS, G)),
            dma((ITERS, G - 1)),
            dma((ITERS, G)),
            dma((ITERS, SIDE - 1)),
            dma((ITERS, SIDE)),
            dma((ITERS, SIDE - 1)),
            dma((ITERS, SIDE)),
        ],
        compiler_params=pltpu.CompilerParams(
            collective_id=0, has_side_effects=True, vmem_limit_bytes=40 * 1024 * 1024
        ),
        name="subspace",
    )(
        block_columns[:, :, 0],
        block_counts[:, :, 0],
        affinity[:, :, 0],
        inv_degree[0],
        panel[0],
    )
    return out[None]


def solution(mesh):
    return jax.shard_map(
        body,
        mesh=mesh,
        in_specs=(
            P(None, "rows", "cols", None, None),
            P(None, "rows", "cols", None),
            P(None, "rows", "cols"),
            P("cols", "rows", None),
            P("cols", "rows", None),
        ),
        out_specs=P("cols", "rows", None),
        check_vma=False,
    )
```

```python
import functools

import jax
import jax.numpy as jnp
from jax import lax
from jax.experimental import pallas as pl
from jax.experimental.pallas import tpu as pltpu
from jax.sharding import PartitionSpec as P

ITERS = 2
SIDE = 4
B = 64
G = 8
R = 8
S = 8
H = B // 2
LANES = 128
NB = 128
MESH = pl.DeviceIdType.MESH
HIGHEST = lax.Precision.HIGHEST
F32 = jnp.float32
BF16 = jnp.bfloat16


def low_lanes(rows):
    return lax.broadcasted_iota(jnp.int32, (rows, LANES), 1) < B


def trade(u, v, low):
    crossed = pltpu.roll(jnp.where(low, v, u), B, 1)
    return jnp.where(low, u, crossed), jnp.where(low, crossed, v)


def inverse_factor(gram):
    row = lax.broadcasted_iota(jnp.int32, (B, LANES), 0)
    lane = lax.broadcasted_iota(jnp.int32, (B, LANES), 1)
    m = jnp.where(lane < B, gram, jnp.where(lane - B == row, 1.0, 0.0).astype(F32))
    done = []
    for block in range(B // 8):
        height = B - 8 * block
        rows = lax.broadcasted_iota(jnp.int32, (height, LANES), 0)
        columns = [
            jnp.broadcast_to(m[:, 8 * block + j : 8 * block + j + 1], (height, LANES))
            for j in range(8)
        ]
        for j in range(8):
            ratio = columns[j] * (1.0 / columns[j][j : j + 1, :])
            ratio = jnp.where(rows > j, ratio, 0.0)
            for later in range(j + 1, 8):
                columns[later] = columns[later] - ratio * columns[later][j : j + 1, :]
            m = m - ratio * m[j : j + 1, :]
        done.append(m[:8])
        m = m[8:]
    m = jnp.concatenate(done, axis=0)
    pivots = jnp.sum(jnp.where(lane == row, m, 0.0), axis=1, keepdims=True)
    return m * lax.rsqrt(pivots)


def twice(inverse):
    low = low_lanes(B)
    upper = jnp.where(low, pltpu.roll(inverse, B, 1), 0.0)
    lower = jnp.where(low, 0.0, inverse)
    return jnp.concatenate([upper, lower], axis=0)


def times_transpose(rows, factor):
    return lax.dot_general(
        rows, factor, (((1,), (1,)), ((), ())), precision=HIGHEST, preferred_element_type=F32
    )


def kernel(
    total_rows,
    columns_hbm, counts_hbm, affinity_ref, inverse_hbm, panel_hbm,
    out_ref,
    columns_ref, counts_ref, inverse_ref, panel_ref,
    raw, blocks, stage, degree, rows_ref, pack, gathered, table, crossing, crossed, partial,
    outgoing, incoming, gram_z, gram_p,
    in_sem, raw_sem, ag_send, ag_recv, core_send, core_recv, rs_send, rs_recv, gz_send, gz_recv, gp_send, gp_recv,
):
    mine_r, mine_c = lax.axis_index("rows"), lax.axis_index("cols")
    x, y = mine_r // SIDE, lax.rem(mine_r, SIDE)
    z, core = mine_c // 2, lax.rem(mine_c, 2)

    def row_of(dx, dy):
        return lax.rem(x + dx + SIDE, SIDE) * SIDE + lax.rem(y + dy + SIDE, SIDE)

    def col_of(dz, dc):
        return lax.rem(z + dz, SIDE) * 2 + lax.rem(core + dc, 2)

    x_peers = [row_of(d, 0) for d in (2, 1, 3)]
    y_peers = [row_of(0, d) for d in (2, 1, 3)]
    order = [(2, 0), (2, 1), (1, 0), (3, 0), (1, 1), (3, 1), (0, 1)]
    z_peers = [col_of(*d) for d in order]
    plane = [row_of(dx, dy) for dx, dy in ((2, 2), (2, 1), (2, 3), (1, 2), (3, 2), (2, 0), (0, 2))]
    plane += [row_of(dx, dy) for dx in (1, 3) for dy in (1, 3)] + [row_of(*d) for d in ((1, 0), (3, 0), (0, 1), (0, 3))]

    arrivals = [
        pltpu.make_async_copy(source, target, in_sem.at[n])
        for n, (source, target) in enumerate(
            (
                (panel_hbm, panel_ref),
                (inverse_hbm, inverse_ref),
                (columns_hbm, columns_ref),
                (counts_hbm, counts_ref),
            )
        )
    ]
    for arrival in arrivals:
        arrival.start()
    for g in range(G):
        pltpu.make_async_copy(affinity_ref.at[g], raw.at[g], raw_sem.at[g]).start()

    barrier = pltpu.get_barrier_semaphore()
    for peer in x_peers + y_peers:
        pl.semaphore_signal(barrier, inc=1, device_id={"rows": peer}, device_id_type=MESH)
    for peer in z_peers:
        pl.semaphore_signal(barrier, inc=1, device_id={"cols": peer}, device_id_type=MESH)

    for arrival in arrivals:
        arrival.wait()

    spread = lax.broadcasted_iota(jnp.int32, (H, B), 1) // 2 == lax.broadcasted_iota(jnp.int32, (H, B), 0)
    picked = jnp.concatenate(
        [jnp.where(spread, jnp.broadcast_to(inverse_ref[i : i + 1, :], (H, B)), 0.0) for i in range(R)], axis=0
    )
    halves = (
        lax.rem(lax.broadcasted_iota(jnp.int32, (B, LANES), 0), 2)
        == lax.broadcasted_iota(jnp.int32, (B, LANES), 1) // B
    )
    degree[...] = jnp.dot(
        picked, jnp.where(halves, 1.0, 0.0).astype(F32), precision=HIGHEST, preferred_element_type=F32
    )
    for t in range(H):
        rows_ref[pl.ds(t, R, stride=H), :] = panel_ref[:, t * LANES : (t + 1) * LANES]

    low_h = low_lanes(H)
    low_b = low_lanes(B)

    def fill_own(it):
        for pair in range(4):
            rows = slice(2 * pair * H, 2 * pair * H + B)
            scaled = rows_ref[rows, :] * degree[rows, :]
            even, odd = trade(scaled[:H], scaled[H:], low_h)
            pack[pl.ds(pair * B, H, stride=2), :] = even
            pack[pl.ds(pair * B + 1, H, stride=2), :] = odd
            gathered[it, mine_r * 4 + pair] = pack[pair * B : (pair + 1) * B, :].astype(BF16)

    def ag_copy(it, slot, number, peer):
        both = pl.ds(2 * slot, 2)
        return pltpu.make_async_remote_copy(
            src_ref=gathered.at[it, both],
            dst_ref=gathered.at[it, both],
            send_sem=ag_send.at[it, number],
            recv_sem=ag_recv.at[it, slot],
            device_id={"rows": peer},
            device_id_type=MESH,
        )

    pending = []

    def expand(it, slot):
        pair = gathered[it, slot]
        zero = jnp.zeros_like(pair)
        table[2 * slot] = jnp.where(low_b, pair, zero)
        table[2 * slot + 1] = jnp.where(low_b, zero, pair)

    def all_gather(it, meanwhile):
        sent = [0]

        def slot_of(dx, dy, half):
            return row_of(dx, dy) * 2 + half

        def send(dx, dy, half, peers):
            for peer in peers:
                copy = ag_copy(it, slot_of(dx, dy, half), sent[0], peer)
                sent[0] += 1
                copy.start()
                pending.append(copy)

        def take(dx, dy, half, peers=()):
            slot = slot_of(dx, dy, half)
            ag_copy(it, slot, 0, mine_r).wait_recv()
            send(dx, dy, half, peers)
            for pair in range(2):
                expand(it, 2 * slot + pair)

        for peer_x, peer_y in zip(x_peers, y_peers):
            send(0, 0, 0, (peer_x,))
            send(0, 0, 1, (peer_y,))
        send(0, 0, 0, y_peers)
        send(0, 0, 1, x_peers)
        for pair in range(4):
            expand(it, mine_r * 4 + pair)
        meanwhile(0)
        for d in (-1, 1):
            take(d, 0, 0, y_peers)
            take(0, d, 1, x_peers)
        meanwhile(1)
        take(2, 0, 0, y_peers)
        take(0, 2, 1, x_peers)
        meanwhile(2)
        for d in (-1, 1, 2):
            take(0, d, 0)
            take(d, 0, 1)
        meanwhile(3)
        for d in (-1, 1, 2):
            for e in (-1, 1, 2):
                take(e, d, 0)
                take(d, e, 1)

    def arrange(g):
        pltpu.make_async_copy(affinity_ref.at[g], raw.at[g], raw_sem.at[g]).wait()

        def one(i, carry):
            for t in range(H):
                stage[pl.ds(t, S, stride=H), :] = raw[g, i, :, t * LANES : (t + 1) * LANES].astype(F32)
            for u in range(S // 2):
                upper, lower = trade(
                    stage[2 * u * H : (2 * u + 1) * H, :], stage[(2 * u + 1) * H : (2 * u + 2) * H, :], low_h
                )
                blocks[g * R + i, 0:H, u * LANES : (u + 1) * LANES] = upper.astype(BF16)
                blocks[g * R + i, H:B, u * LANES : (u + 1) * LANES] = lower.astype(BF16)
            return carry

        lax.fori_loop(0, R, one, 0)

    def product(g, i):
        count = counts_ref[g, i]
        right = []
        for s in range(S):
            column = jnp.where(s < count, columns_ref[g, i, s], NB)
            right.append(table[column])
        o = jnp.dot(blocks[g * R + i], jnp.concatenate(right, axis=0), preferred_element_type=F32)
        even, odd = o[:H], o[H:]
        return jnp.where(low_h, even, odd) + pltpu.roll(jnp.where(low_h, odd, even), B, 1)

    partner = col_of(0, 1)
    chips = (2, 1, 3, 0)

    def core_copy(it, k):
        return pltpu.make_async_remote_copy(
            src_ref=crossing.at[it, k],
            dst_ref=crossed.at[it, k],
            send_sem=core_send.at[it, k],
            recv_sem=core_recv.at[it, k],
            device_id={"cols": partner},
            device_id_type=MESH,
        )

    def rs_copy(it, k, slot, peer):
        return pltpu.make_async_remote_copy(
            src_ref=outgoing.at[it, k],
            dst_ref=incoming.at[it, slot],
            send_sem=rs_send.at[it, k],
            recv_sem=rs_recv.at[it, slot],
            device_id={"cols": peer},
            device_id_type=MESH,
        )

    UNROLL = 4

    def products(g, put):
        def some(step, carry):
            for j in range(UNROLL):
                i = step * UNROLL + j
                put(pl.ds(pl.multiple_of(i * H, H), H), product(g, i))
            return carry

        lax.fori_loop(0, R // UNROLL, some, 0)

    def multiply(it):
        def pass_on(k):
            core_copy(it, k).wait_recv()
            outgoing[it, k] = (partial[k] + crossed[it, k].astype(F32)).astype(BF16)
            copy = rs_copy(it, k, z, col_of(chips[k], 0))
            copy.start()
            pending.append(copy)

        for k, dz in enumerate(chips):
            def put_crossing(at, value, k=k):
                crossing[it, k, at, :] = value.astype(BF16)

            def put_partial(at, value, k=k):
                partial[k, at, :] = value

            products(col_of(dz, 1), put_crossing)
            copy = core_copy(it, k)
            copy.start()
            pending.append(copy)
            products(col_of(dz, 0), put_partial)
            if k:
                pass_on(k - 1)

    def collect(it):
        core_copy(it, 3).wait_recv()
        summed = partial[3] + crossed[it, 3].astype(F32)
        for k in range(3):
            slot = lax.rem(z + chips[k], SIDE)
            rs_copy(it, k, slot, partner).wait_recv()
            summed = summed + incoming[it, slot].astype(F32)
        return summed * degree[...]

    def exchange(it, buffer, send_sem, recv_sem, at, axis, peers, slots):
        def copy(n, slot):
            return pltpu.make_async_remote_copy(
                src_ref=buffer.at[it, at],
                dst_ref=buffer.at[it, slot],
                send_sem=send_sem.at[it, n],
                recv_sem=recv_sem.at[it, slot],
                device_id={axis: peers[n]},
                device_id_type=MESH,
            )

        def start():
            for n in range(len(peers)):
                c = copy(n, at)
                c.start()
                pending.append(c)

        def finish():
            for n in range(len(peers)):
                copy(n, slots[n]).wait_recv()
            total = buffer[it, 0]
            for n in range(1, len(peers) + 1):
                total = total + buffer[it, n]
            return total

        return start, finish

    def gram_of(it):
        along_z = exchange(it, gram_z, gz_send, gz_recv, mine_c, "cols", z_peers, z_peers)
        along_plane = exchange(it, gram_p, gp_send, gp_recv, mine_r, "rows", plane, plane)

        def first():
            rows = rows_ref[...]
            both = lax.dot_general(
                rows, rows, (((0,), (0,)), ((), ())), precision=HIGHEST, preferred_element_type=F32
            )
            gram = both[:B] + pltpu.roll(both[B:], B, 1)
            gram_z[it, mine_c] = jnp.where(low_h, gram[:H], pltpu.roll(gram[H:], B, 1))
            along_z[0]()

        def second():
            gram_p[it, mine_r] = along_z[1]()
            along_plane[0]()

        def last():
            total = along_plane[1]() * (1.0 / total_rows)
            return jnp.concatenate([total, pltpu.roll(total, B, 1)], axis=0)

        return first, second, last

    fill_own(0)
    table[NB] = jnp.zeros((B, LANES), BF16)
    pl.semaphore_wait(barrier, len(x_peers) + len(y_peers) + len(z_peers))

    shares = [(0, 1), (2,), (3, 4), (5, 6, 7)]

    def arranging(n):
        for g in shares[n]:
            arrange(g)

    all_gather(0, arranging)
    multiply(0)
    rows_ref[...] = collect(0)

    first, second, last = gram_of(0)
    fill_own(1)

    def reducing(n):
        if n == 0:
            first()
        elif n == 3:
            second()

    all_gather(1, reducing)
    multiply(1)
    factor = twice(inverse_factor(last()))
    rows_ref[...] = times_transpose(collect(1), factor)

    first, second, last = gram_of(1)
    first()
    second()
    factor = twice(inverse_factor(last()))
    rows_ref[...] = times_transpose(rows_ref[...], factor)
    for t in range(H):
        out_ref[:, t * LANES : (t + 1) * LANES] = rows_ref[pl.ds(t, R, stride=H), :]
    for copy in pending:
        copy.wait_send()


def body(affinity, block_columns, block_counts, inv_degree, panel):
    total_rows = float(affinity.shape[0] * affinity.shape[1] * lax.axis_size("rows") * B)
    dma = pltpu.SemaphoreType.DMA
    out = pl.pallas_call(
        functools.partial(kernel, total_rows),
        out_shape=jax.ShapeDtypeStruct((R, H * LANES), F32),
        in_specs=[
            pl.BlockSpec(memory_space=pltpu.HBM),
        ]
        * 5,
        out_specs=pl.BlockSpec(memory_space=pltpu.VMEM),
        scratch_shapes=[
            pltpu.SMEM((G, R, S), jnp.int32),
            pltpu.SMEM((G, R), jnp.int32),
            pltpu.VMEM((R, B), F32),
            pltpu.VMEM((R, H * LANES), F32),
            pltpu.VMEM((G, R, S, H * LANES), BF16),
            pltpu.VMEM((G * R, B, S * B), BF16),
            pltpu.VMEM((S * H, LANES), F32),
            pltpu.VMEM((R * H, LANES), F32),
            pltpu.VMEM((R * H, LANES), F32),
            pltpu.VMEM((R * H, LANES), F32),
            pltpu.VMEM((ITERS, NB // 2, B, LANES), BF16),
            pltpu.VMEM((NB + 1, B, LANES), BF16),
            pltpu.VMEM((ITERS, SIDE, R * H, LANES), BF16),
            pltpu.VMEM((ITERS, SIDE, R * H, LANES), BF16),
            pltpu.VMEM((SIDE, R * H, LANES), F32),
            pltpu.VMEM((ITERS, SIDE - 1, R * H, LANES), BF16),
            pltpu.VMEM((ITERS, SIDE, R * H, LANES), BF16),
            pltpu.VMEM((ITERS, G, H, LANES), F32),
            pltpu.VMEM((ITERS, SIDE * SIDE, H, LANES), F32),
            dma((4,)),
            dma((G,)),
            dma((ITERS, 30)),
            dma((ITERS, 2 * SIDE * SIDE)),
            dma((ITERS, SIDE)),
            dma((ITERS, SIDE)),
            dma((ITERS, SIDE - 1)),
            dma((ITERS, SIDE)),
            dma((ITERS, G - 1)),
            dma((ITERS, G)),
            dma((ITERS, SIDE * SIDE - 1)),
            dma((ITERS, SIDE * SIDE)),
        ],
        compiler_params=pltpu.CompilerParams(
            collective_id=0, has_side_effects=True, vmem_limit_bytes=60 * 1024 * 1024
        ),
        name="subspace",
    )(
        block_columns[:, :, 0],
        block_counts[:, :, 0],
        affinity[:, :, 0],
        inv_degree[0],
        panel[0],
    )
    return out[None]


def solution(mesh):
    return jax.shard_map(
        body,
        mesh=mesh,
        in_specs=(
            P(None, "rows", "cols", None, None),
            P(None, "rows", "cols", None),
            P(None, "rows", "cols"),
            P("cols", "rows", None),
            P("cols", "rows", None),
        ),
        out_specs=P("cols", "rows", None),
        check_vma=False,
    )
```

```python
import functools

import jax
import jax.numpy as jnp
from jax import lax
from jax.experimental import pallas as pl
from jax.experimental.pallas import tpu as pltpu
from jax.sharding import PartitionSpec as P

ITERS = 2
SIDE = 4
B = 64
G = 8
R = 8
S = 8
H = B // 2
LANES = 128
NB = 128
MESH = pl.DeviceIdType.MESH
HIGHEST = lax.Precision.HIGHEST
F32 = jnp.float32
BF16 = jnp.bfloat16


def low_lanes(rows):
    return lax.broadcasted_iota(jnp.int32, (rows, LANES), 1) < B


def trade(u, v, low):
    crossed = pltpu.roll(jnp.where(low, v, u), B, 1)
    return jnp.where(low, u, crossed), jnp.where(low, crossed, v)


def inverse_factor(gram):
    row = lax.broadcasted_iota(jnp.int32, (B, LANES), 0)
    lane = lax.broadcasted_iota(jnp.int32, (B, LANES), 1)
    m = jnp.where(lane < B, gram, jnp.where(lane - B == row, 1.0, 0.0).astype(F32))
    done = []
    for block in range(B // 8):
        height = B - 8 * block
        rows = lax.broadcasted_iota(jnp.int32, (height, LANES), 0)
        columns = [
            jnp.broadcast_to(m[:, 8 * block + j : 8 * block + j + 1], (height, LANES))
            for j in range(8)
        ]
        for j in range(8):
            ratio = columns[j] * (1.0 / columns[j][j : j + 1, :])
            ratio = jnp.where(rows > j, ratio, 0.0)
            for later in range(j + 1, 8):
                columns[later] = columns[later] - ratio * columns[later][j : j + 1, :]
            m = m - ratio * m[j : j + 1, :]
        done.append(m[:8])
        m = m[8:]
    m = jnp.concatenate(done, axis=0)
    pivots = jnp.sum(jnp.where(lane == row, m, 0.0), axis=1, keepdims=True)
    return m * lax.rsqrt(pivots)


def twice(inverse):
    low = low_lanes(B)
    upper = jnp.where(low, pltpu.roll(inverse, B, 1), 0.0)
    lower = jnp.where(low, 0.0, inverse)
    return jnp.concatenate([upper, lower], axis=0)


def times_transpose(rows, factor):
    return lax.dot_general(
        rows, factor, (((1,), (1,)), ((), ())), precision=HIGHEST, preferred_element_type=F32
    )


def kernel(
    total_rows,
    columns_hbm, counts_hbm, affinity_ref, inverse_hbm, panel_hbm,
    out_ref,
    columns_ref, counts_ref, index_ref, inverse_ref, panel_ref,
    raw, blocks, stage, degree, rows_ref, pack, gathered, table, crossing, crossed, partial,
    outgoing, incoming, gram_z, gram_p,
    in_sem, raw_sem, ag_send, ag_recv, core_send, core_recv, rs_send, rs_recv, gz_send, gz_recv, gp_send, gp_recv,
):
    mine_r, mine_c = lax.axis_index("rows"), lax.axis_index("cols")
    x, y = mine_r // SIDE, lax.rem(mine_r, SIDE)
    z, core = mine_c // 2, lax.rem(mine_c, 2)

    def row_of(dx, dy):
        return lax.rem(x + dx + SIDE, SIDE) * SIDE + lax.rem(y + dy + SIDE, SIDE)

    def col_of(dz, dc):
        return lax.rem(z + dz, SIDE) * 2 + lax.rem(core + dc, 2)

    x_peers = [row_of(d, 0) for d in (2, 1, 3)]
    y_peers = [row_of(0, d) for d in (2, 1, 3)]
    order = [(2, 0), (2, 1), (1, 0), (3, 0), (1, 1), (3, 1), (0, 1)]
    z_peers = [col_of(*d) for d in order]
    plane = [row_of(dx, dy) for dx, dy in ((2, 2), (2, 1), (2, 3), (1, 2), (3, 2), (2, 0), (0, 2))]
    plane += [row_of(dx, dy) for dx in (1, 3) for dy in (1, 3)] + [row_of(*d) for d in ((1, 0), (3, 0), (0, 1), (0, 3))]

    arrivals = [
        pltpu.make_async_copy(source, target, in_sem.at[n])
        for n, (source, target) in enumerate(
            (
                (panel_hbm, panel_ref),
                (inverse_hbm, inverse_ref),
                (columns_hbm, columns_ref),
                (counts_hbm, counts_ref),
            )
        )
    ]
    for arrival in arrivals:
        arrival.start()
    for g in range(G):
        pltpu.make_async_copy(affinity_ref.at[g], raw.at[g], raw_sem.at[g]).start()

    barrier = pltpu.get_barrier_semaphore()
    for peer in x_peers + y_peers:
        pl.semaphore_signal(barrier, inc=1, device_id={"rows": peer}, device_id_type=MESH)
    for peer in z_peers:
        pl.semaphore_signal(barrier, inc=1, device_id={"cols": peer}, device_id_type=MESH)

    for arrival in arrivals:
        arrival.wait()

    spread = lax.broadcasted_iota(jnp.int32, (H, B), 1) // 2 == lax.broadcasted_iota(jnp.int32, (H, B), 0)
    picked = jnp.concatenate(
        [jnp.where(spread, jnp.broadcast_to(inverse_ref[i : i + 1, :], (H, B)), 0.0) for i in range(R)], axis=0
    )
    halves = (
        lax.rem(lax.broadcasted_iota(jnp.int32, (B, LANES), 0), 2)
        == lax.broadcasted_iota(jnp.int32, (B, LANES), 1) // B
    )
    degree[...] = jnp.dot(
        picked, jnp.where(halves, 1.0, 0.0).astype(F32), precision=HIGHEST, preferred_element_type=F32
    )
    for t in range(H):
        rows_ref[pl.ds(t, R, stride=H), :] = panel_ref[:, t * LANES : (t + 1) * LANES]

    low_h = low_lanes(H)
    low_b = low_lanes(B)

    def fill_own(it):
        for pair in range(4):
            rows = slice(2 * pair * H, 2 * pair * H + B)
            scaled = rows_ref[rows, :] * degree[rows, :]
            even, odd = trade(scaled[:H], scaled[H:], low_h)
            pack[pl.ds(pair * B, H, stride=2), :] = even
            pack[pl.ds(pair * B + 1, H, stride=2), :] = odd
            gathered[it, mine_r * 4 + pair] = pack[pair * B : (pair + 1) * B, :].astype(BF16)

    def ag_copy(it, slot, number, peer):
        both = pl.ds(2 * slot, 2)
        return pltpu.make_async_remote_copy(
            src_ref=gathered.at[it, both],
            dst_ref=gathered.at[it, both],
            send_sem=ag_send.at[it, number],
            recv_sem=ag_recv.at[it, slot],
            device_id={"rows": peer},
            device_id_type=MESH,
        )

    pending = []

    def expand(it, slot):
        pair = gathered[it, slot]
        zero = jnp.zeros_like(pair)
        table[2 * slot] = jnp.where(low_b, pair, zero)
        table[2 * slot + 1] = jnp.where(low_b, zero, pair)

    def all_gather(it, meanwhile):
        sent = [0]

        def slot_of(dx, dy, half):
            return row_of(dx, dy) * 2 + half

        def send(dx, dy, half, peers):
            for peer in peers:
                copy = ag_copy(it, slot_of(dx, dy, half), sent[0], peer)
                sent[0] += 1
                copy.start()
                pending.append(copy)

        def take(dx, dy, half, peers=()):
            slot = slot_of(dx, dy, half)
            ag_copy(it, slot, 0, mine_r).wait_recv()
            send(dx, dy, half, peers)
            for pair in range(2):
                expand(it, 2 * slot + pair)

        for peer_x, peer_y in zip(x_peers, y_peers):
            send(0, 0, 0, (peer_x,))
            send(0, 0, 1, (peer_y,))
        send(0, 0, 0, y_peers)
        send(0, 0, 1, x_peers)
        for pair in range(4):
            expand(it, mine_r * 4 + pair)
        meanwhile(0)
        for d in (-1, 1):
            take(d, 0, 0, y_peers)
            take(0, d, 1, x_peers)
        meanwhile(1)
        take(2, 0, 0, y_peers)
        take(0, 2, 1, x_peers)
        meanwhile(2)
        for d in (-1, 1, 2):
            take(0, d, 0)
            take(d, 0, 1)
        meanwhile(3)
        for d in (-1, 1, 2):
            for e in (-1, 1, 2):
                take(e, d, 0)
                take(d, e, 1)

    def arrange(g):
        pltpu.make_async_copy(affinity_ref.at[g], raw.at[g], raw_sem.at[g]).wait()

        def one(i, carry):
            count = counts_ref[g, i]
            for s in range(S):
                index_ref[(g * R + i) * S + s] = jnp.where(s < count, columns_ref[g, i, s], NB)
            for t in range(H):
                stage[pl.ds(t, S, stride=H), :] = raw[g, i, :, t * LANES : (t + 1) * LANES].astype(F32)
            for u in range(S // 2):
                upper, lower = trade(
                    stage[2 * u * H : (2 * u + 1) * H, :], stage[(2 * u + 1) * H : (2 * u + 2) * H, :], low_h
                )
                blocks[g * R + i, 0:H, u * LANES : (u + 1) * LANES] = upper.astype(BF16)
                blocks[g * R + i, H:B, u * LANES : (u + 1) * LANES] = lower.astype(BF16)
            return carry

        lax.fori_loop(0, R, one, 0)

    def gathered_blocks(g, i):
        first = (g * R + i) * S
        return jnp.concatenate([table[index_ref[first + s]] for s in range(S)], axis=0)

    def product(g, i):
        left = jnp.concatenate([blocks[g * R + i], blocks[g * R + i + 1]], axis=0)
        right = jnp.concatenate([gathered_blocks(g, i), gathered_blocks(g, i + 1)], axis=1)
        o = jnp.dot(left, right, preferred_element_type=F32)
        terms = []
        for quarter in (o[:B, :LANES], o[B:, LANES:]):
            even, odd = quarter[:H], quarter[H:]
            terms.append(jnp.where(low_h, even, odd) + pltpu.roll(jnp.where(low_h, odd, even), B, 1))
        return jnp.concatenate(terms, axis=0)

    partner = col_of(0, 1)
    chips = (2, 1, 3, 0)

    def core_copy(it, k):
        return pltpu.make_async_remote_copy(
            src_ref=crossing.at[it, k],
            dst_ref=crossed.at[it, k],
            send_sem=core_send.at[it, k],
            recv_sem=core_recv.at[it, k],
            device_id={"cols": partner},
            device_id_type=MESH,
        )

    def rs_copy(it, k, slot, peer):
        return pltpu.make_async_remote_copy(
            src_ref=outgoing.at[it, k],
            dst_ref=incoming.at[it, slot],
            send_sem=rs_send.at[it, k],
            recv_sem=rs_recv.at[it, slot],
            device_id={"cols": peer},
            device_id_type=MESH,
        )

    def products(g, put):
        for i in range(0, R, 2):
            put(slice(i * H, i * H + B), product(g, i))

    def multiply(it):
        def pass_on(k):
            core_copy(it, k).wait_recv()
            outgoing[it, k] = (partial[k] + crossed[it, k].astype(F32)).astype(BF16)
            copy = rs_copy(it, k, z, col_of(chips[k], 0))
            copy.start()
            pending.append(copy)

        def cross(k):
            def put(at, value):
                crossing[it, k, at, :] = value.astype(BF16)

            products(col_of(chips[k], 1), put)
            copy = core_copy(it, k)
            copy.start()
            pending.append(copy)

        def keep(k):
            def put(at, value):
                partial[k, at, :] = value

            products(col_of(chips[k], 0), put)

        cross(0)
        cross(1)
        keep(0)
        pass_on(0)
        cross(2)
        keep(1)
        pass_on(1)
        keep(2)
        pass_on(2)
        cross(3)
        keep(3)

    def collect(it):
        core_copy(it, 3).wait_recv()
        summed = partial[3] + crossed[it, 3].astype(F32)
        for k in range(3):
            slot = lax.rem(z + chips[k], SIDE)
            rs_copy(it, k, slot, partner).wait_recv()
            summed = summed + incoming[it, slot].astype(F32)
        return summed * degree[...]

    def exchange(it, buffer, send_sem, recv_sem, at, axis, peers, slots):
        def copy(n, slot):
            return pltpu.make_async_remote_copy(
                src_ref=buffer.at[it, at],
                dst_ref=buffer.at[it, slot],
                send_sem=send_sem.at[it, n],
                recv_sem=recv_sem.at[it, slot],
                device_id={axis: peers[n]},
                device_id_type=MESH,
            )

        def start():
            for n in range(len(peers)):
                c = copy(n, at)
                c.start()
                pending.append(c)

        def finish():
            for n in range(len(peers)):
                copy(n, slots[n]).wait_recv()
            total = buffer[it, 0]
            for n in range(1, len(peers) + 1):
                total = total + buffer[it, n]
            return total

        return start, finish

    def gram_of(it):
        along_z = exchange(it, gram_z, gz_send, gz_recv, mine_c, "cols", z_peers, z_peers)
        along_plane = exchange(it, gram_p, gp_send, gp_recv, mine_r, "rows", plane, plane)

        def first():
            rows = rows_ref[...]
            both = lax.dot_general(
                rows, rows, (((0,), (0,)), ((), ())), precision=HIGHEST, preferred_element_type=F32
            )
            gram = both[:B] + pltpu.roll(both[B:], B, 1)
            gram_z[it, mine_c] = jnp.where(low_h, gram[:H], pltpu.roll(gram[H:], B, 1))
            along_z[0]()

        def second():
            gram_p[it, mine_r] = along_z[1]()
            along_plane[0]()

        def last():
            total = along_plane[1]() * (1.0 / total_rows)
            return jnp.concatenate([total, pltpu.roll(total, B, 1)], axis=0)

        return first, second, last

    fill_own(0)
    table[NB] = jnp.zeros((B, LANES), BF16)
    pl.semaphore_wait(barrier, len(x_peers) + len(y_peers) + len(z_peers))

    shares = [(0, 1), (2,), (3, 4), (5, 6, 7)]

    def arranging(n):
        for g in shares[n]:
            arrange(g)

    all_gather(0, arranging)
    multiply(0)
    rows_ref[...] = collect(0)

    first, second, last = gram_of(0)
    fill_own(1)

    all_gather(1, lambda n: n == 0 and first())
    second()
    multiply(1)
    factor = twice(inverse_factor(last()))
    rows_ref[...] = times_transpose(collect(1), factor)

    first, second, last = gram_of(1)
    first()
    second()
    factor = twice(inverse_factor(last()))
    rows_ref[...] = times_transpose(rows_ref[...], factor)
    for t in range(H):
        out_ref[:, t * LANES : (t + 1) * LANES] = rows_ref[pl.ds(t, R, stride=H), :]
    for copy in pending:
        copy.wait_send()


def body(affinity, block_columns, block_counts, inv_degree, panel):
    total_rows = float(affinity.shape[0] * affinity.shape[1] * lax.axis_size("rows") * B)
    dma = pltpu.SemaphoreType.DMA
    out = pl.pallas_call(
        functools.partial(kernel, total_rows),
        out_shape=jax.ShapeDtypeStruct((R, H * LANES), F32),
        in_specs=[
            pl.BlockSpec(memory_space=pltpu.HBM),
        ]
        * 5,
        out_specs=pl.BlockSpec(memory_space=pltpu.VMEM),
        scratch_shapes=[
            pltpu.SMEM((G, R, S), jnp.int32),
            pltpu.SMEM((G, R), jnp.int32),
            pltpu.SMEM((G * R * S,), jnp.int32),
            pltpu.VMEM((R, B), F32),
            pltpu.VMEM((R, H * LANES), F32),
            pltpu.VMEM((G, R, S, H * LANES), BF16),
            pltpu.VMEM((G * R, B, S * B), BF16),
            pltpu.VMEM((S * H, LANES), F32),
            pltpu.VMEM((R * H, LANES), F32),
            pltpu.VMEM((R * H, LANES), F32),
            pltpu.VMEM((R * H, LANES), F32),
            pltpu.VMEM((ITERS, NB // 2, B, LANES), BF16),
            pltpu.VMEM((NB + 1, B, LANES), BF16),
            pltpu.VMEM((ITERS, SIDE, R * H, LANES), BF16),
            pltpu.VMEM((ITERS, SIDE, R * H, LANES), BF16),
            pltpu.VMEM((SIDE, R * H, LANES), F32),
            pltpu.VMEM((ITERS, SIDE - 1, R * H, LANES), BF16),
            pltpu.VMEM((ITERS, SIDE, R * H, LANES), BF16),
            pltpu.VMEM((ITERS, G, H, LANES), F32),
            pltpu.VMEM((ITERS, SIDE * SIDE, H, LANES), F32),
            dma((4,)),
            dma((G,)),
            dma((ITERS, 30)),
            dma((ITERS, 2 * SIDE * SIDE)),
            dma((ITERS, SIDE)),
            dma((ITERS, SIDE)),
            dma((ITERS, SIDE - 1)),
            dma((ITERS, SIDE)),
            dma((ITERS, G - 1)),
            dma((ITERS, G)),
            dma((ITERS, SIDE * SIDE - 1)),
            dma((ITERS, SIDE * SIDE)),
        ],
        compiler_params=pltpu.CompilerParams(
            collective_id=0, has_side_effects=True, vmem_limit_bytes=60 * 1024 * 1024
        ),
        name="subspace",
    )(
        block_columns[:, :, 0],
        block_counts[:, :, 0],
        affinity[:, :, 0],
        inv_degree[0],
        panel[0],
    )
    return out[None]


def solution(mesh):
    return jax.shard_map(
        body,
        mesh=mesh,
        in_specs=(
            P(None, "rows", "cols", None, None),
            P(None, "rows", "cols", None),
            P(None, "rows", "cols"),
            P("cols", "rows", None),
            P("cols", "rows", None),
        ),
        out_specs=P("cols", "rows", None),
        check_vma=False,
    )
```

```python
import functools

import jax
import jax.numpy as jnp
from jax import lax
from jax.experimental import pallas as pl
from jax.experimental.pallas import tpu as pltpu
from jax.sharding import PartitionSpec as P

ITERS = 2
SIDE = 4
B = 64
G = 8
R = 8
S = 8
H = B // 2
LANES = 128
NB = 128
DISTANCES = (2, 1, 3)
MESH = pl.DeviceIdType.MESH
HIGHEST = lax.Precision.HIGHEST
F32 = jnp.float32
BF16 = jnp.bfloat16


def low_lanes(rows):
    return lax.broadcasted_iota(jnp.int32, (rows, LANES), 1) < B


def trade(u, v, low):
    crossed = pltpu.roll(jnp.where(low, v, u), B, 1)
    return jnp.where(low, u, crossed), jnp.where(low, crossed, v)


def inverse_factor(gram):
    row = lax.broadcasted_iota(jnp.int32, (B, LANES), 0)
    lane = lax.broadcasted_iota(jnp.int32, (B, LANES), 1)
    m = jnp.where(lane < B, gram, jnp.where(lane - B == row, 1.0, 0.0).astype(F32))
    done = []
    for block in range(B // 8):
        height = B - 8 * block
        rows = lax.broadcasted_iota(jnp.int32, (height, LANES), 0)
        columns = [
            jnp.broadcast_to(m[:, 8 * block + j : 8 * block + j + 1], (height, LANES))
            for j in range(8)
        ]
        for j in range(8):
            ratio = columns[j] * (1.0 / columns[j][j : j + 1, :])
            ratio = jnp.where(rows > j, ratio, 0.0)
            for later in range(j + 1, 8):
                columns[later] = columns[later] - ratio * columns[later][j : j + 1, :]
            m = m - ratio * m[j : j + 1, :]
        done.append(m[:8])
        m = m[8:]
    m = jnp.concatenate(done, axis=0)
    pivots = jnp.sum(jnp.where(lane == row, m, 0.0), axis=1, keepdims=True)
    return m * lax.rsqrt(pivots)


def twice(inverse):
    low = low_lanes(B)
    upper = jnp.where(low, pltpu.roll(inverse, B, 1), 0.0)
    lower = jnp.where(low, 0.0, inverse)
    return jnp.concatenate([upper, lower], axis=0)


def times_transpose(rows, factor):
    return lax.dot_general(
        rows, factor, (((1,), (1,)), ((), ())), precision=HIGHEST, preferred_element_type=F32
    )


def kernel(
    total_rows,
    columns_hbm, counts_hbm, affinity_ref, inverse_hbm, panel_hbm,
    out_ref,
    columns_ref, counts_ref, index_ref, inverse_ref, panel_ref,
    raw, blocks, stage, degree, rows_ref, pack, gathered, table, crossing, crossed, partial,
    outgoing, incoming, gram_z, gram_p,
    in_sem, raw_sem, ag_send, ag_recv, core_send, core_recv, rs_send, rs_recv, gz_send, gz_recv, gp_send, gp_recv,
):
    mine_r, mine_c = lax.axis_index("rows"), lax.axis_index("cols")
    x, y = mine_r // SIDE, lax.rem(mine_r, SIDE)
    z, core = mine_c // 2, lax.rem(mine_c, 2)

    def row_of(dx, dy):
        return lax.rem(x + dx + SIDE, SIDE) * SIDE + lax.rem(y + dy + SIDE, SIDE)

    def col_of(dz, dc):
        return lax.rem(z + dz, SIDE) * 2 + lax.rem(core + dc, 2)

    x_peers = [row_of(d, 0) for d in DISTANCES]
    y_peers = [row_of(0, d) for d in DISTANCES]
    order = [(2, 0), (2, 1), (1, 0), (3, 0), (1, 1), (3, 1), (0, 1)]
    z_peers = [col_of(*d) for d in order]
    plane = [row_of(dx, dy) for dx, dy in ((2, 2), (2, 1), (2, 3), (1, 2), (3, 2), (2, 0), (0, 2))]
    plane += [row_of(dx, dy) for dx in (1, 3) for dy in (1, 3)] + [row_of(*d) for d in ((1, 0), (3, 0), (0, 1), (0, 3))]

    arrivals = [
        pltpu.make_async_copy(source, target, in_sem.at[n])
        for n, (source, target) in enumerate(
            (
                (panel_hbm, panel_ref),
                (inverse_hbm, inverse_ref),
                (columns_hbm, columns_ref),
                (counts_hbm, counts_ref),
            )
        )
    ]
    for arrival in arrivals:
        arrival.start()
    for g in range(G):
        pltpu.make_async_copy(affinity_ref.at[g], raw.at[g], raw_sem.at[g]).start()

    barrier = pltpu.get_barrier_semaphore()
    for peer in x_peers + y_peers:
        pl.semaphore_signal(barrier, inc=1, device_id={"rows": peer}, device_id_type=MESH)
    for peer in z_peers:
        pl.semaphore_signal(barrier, inc=1, device_id={"cols": peer}, device_id_type=MESH)

    for arrival in arrivals:
        arrival.wait()

    spread = lax.broadcasted_iota(jnp.int32, (H, B), 1) // 2 == lax.broadcasted_iota(jnp.int32, (H, B), 0)
    picked = jnp.concatenate(
        [jnp.where(spread, jnp.broadcast_to(inverse_ref[i : i + 1, :], (H, B)), 0.0) for i in range(R)], axis=0
    )
    halves = (
        lax.rem(lax.broadcasted_iota(jnp.int32, (B, LANES), 0), 2)
        == lax.broadcasted_iota(jnp.int32, (B, LANES), 1) // B
    )
    degree[...] = jnp.dot(
        picked, jnp.where(halves, 1.0, 0.0).astype(F32), precision=HIGHEST, preferred_element_type=F32
    )
    for t in range(H):
        rows_ref[pl.ds(t, R, stride=H), :] = panel_ref[:, t * LANES : (t + 1) * LANES]

    low_h = low_lanes(H)
    low_b = low_lanes(B)

    def fill_own(it, pair):
        rows = slice(2 * pair * H, 2 * pair * H + B)
        scaled = rows_ref[rows, :] * degree[rows, :]
        even, odd = trade(scaled[:H], scaled[H:], low_h)
        pack[pl.ds(pair * B, H, stride=2), :] = even
        pack[pl.ds(pair * B + 1, H, stride=2), :] = odd
        gathered[it, mine_r * 4 + pair] = pack[pair * B : (pair + 1) * B, :].astype(BF16)

    def ag_copy(it, slot, group, peer):
        both = pl.ds(2 * slot, 2)
        return pltpu.make_async_remote_copy(
            src_ref=gathered.at[it, both],
            dst_ref=gathered.at[it, both],
            send_sem=ag_send.at[it],
            recv_sem=ag_recv.at[it, group],
            device_id={"rows": peer},
            device_id_type=MESH,
        )

    def wait_for(ref, sem):
        pltpu.make_async_copy(ref, ref, sem).wait()

    def expand(it, slot):
        pair = gathered[it, slot]
        zero = jnp.zeros_like(pair)
        table[2 * slot] = jnp.where(low_b, pair, zero)
        table[2 * slot + 1] = jnp.where(low_b, zero, pair)

    def all_gather(it, meanwhile):
        def slot_of(dx, dy, half):
            return row_of(dx, dy) * 2 + half

        def send(dx, dy, half, stage):
            along_y = (half == 0) == (stage == 1)
            for n, peer in enumerate(y_peers if along_y else x_peers):
                ag_copy(it, slot_of(dx, dy, half), 6 * stage + 3 * half + n, peer).start()

        def unpack(dx, dy, half):
            for pair in range(2):
                expand(it, 2 * slot_of(dx, dy, half) + pair)

        def take(n, half):
            d = -DISTANCES[n]
            at = (d, 0) if half == 0 else (0, d)
            wait_for(gathered.at[it, pl.ds(0, 2)], ag_recv.at[it, 3 * half + n])
            send(*at, half, 1)
            return at

        def take_all(n, half):
            d = -DISTANCES[n]
            wait_for(gathered.at[it, pl.ds(0, 2 * SIDE)], ag_recv.at[it, 6 + 3 * half + n])
            for e in range(SIDE):
                at = (e, d) if half == 0 else (d, e)
                unpack(*at, half)

        send(0, 0, 0, 1)
        send(0, 0, 1, 1)
        for half in range(2):
            unpack(0, 0, half)
        meanwhile(0)
        for n in (1, 2):
            for half in range(2):
                at = take(n, half)
                unpack(*at, half)
        meanwhile(1)
        for half in range(2):
            at = take(0, half)
            unpack(*at, half)
        meanwhile(2)
        for n in (1, 2, 0):
            for half in range(2):
                take_all(n, half)
        meanwhile(3)
        wait_for(gathered.at[it, pl.ds(0, 60)], ag_send.at[it])

    def send_own(it, half):
        for n, peer in enumerate(y_peers if half else x_peers):
            ag_copy(it, mine_r * 2 + half, 3 * half + n, peer).start()

    def arrange(g):
        pltpu.make_async_copy(affinity_ref.at[g], raw.at[g], raw_sem.at[g]).wait()

        def one(i, carry):
            count = counts_ref[g, i]
            for s in range(S):
                index_ref[(g * R + i) * S + s] = jnp.where(s < count, columns_ref[g, i, s], NB)
            for t in range(H):
                stage[pl.ds(t, S, stride=H), :] = raw[g, i, :, t * LANES : (t + 1) * LANES].astype(F32)
            for u in range(S // 2):
                upper, lower = trade(
                    stage[2 * u * H : (2 * u + 1) * H, :], stage[(2 * u + 1) * H : (2 * u + 2) * H, :], low_h
                )
                blocks[g * R + i, 0:H, u * LANES : (u + 1) * LANES] = upper.astype(BF16)
                blocks[g * R + i, H:B, u * LANES : (u + 1) * LANES] = lower.astype(BF16)
            return carry

        lax.fori_loop(0, R, one, 0)

    def gathered_blocks(g, i):
        first = (g * R + i) * S
        return jnp.concatenate([table[index_ref[first + s]] for s in range(S)], axis=0)

    def product(g, i):
        left = jnp.concatenate([blocks[g * R + i], blocks[g * R + i + 1]], axis=0)
        right = jnp.concatenate([gathered_blocks(g, i), gathered_blocks(g, i + 1)], axis=1)
        o = jnp.dot(left, right, preferred_element_type=F32)
        terms = []
        for quarter in (o[:B, :LANES], o[B:, LANES:]):
            even, odd = quarter[:H], quarter[H:]
            terms.append(jnp.where(low_h, even, odd) + pltpu.roll(jnp.where(low_h, odd, even), B, 1))
        return jnp.concatenate(terms, axis=0)

    partner = col_of(0, 1)
    chips = (2, 1, 3, 0)

    def core_copy(it, k):
        return pltpu.make_async_remote_copy(
            src_ref=crossing.at[it, k],
            dst_ref=crossed.at[it, k],
            send_sem=core_send.at[it],
            recv_sem=core_recv.at[it, k],
            device_id={"cols": partner},
            device_id_type=MESH,
        )

    def rs_copy(it, k, slot, peer):
        return pltpu.make_async_remote_copy(
            src_ref=outgoing.at[it, k],
            dst_ref=incoming.at[it, slot],
            send_sem=rs_send.at[it],
            recv_sem=rs_recv.at[it],
            device_id={"cols": peer},
            device_id_type=MESH,
        )

    def products(g, put):
        for i in range(0, R, 2):
            put(slice(i * H, i * H + B), product(g, i))

    def multiply(it):
        def pass_on(k):
            core_copy(it, k).wait_recv()
            outgoing[it, k] = (partial[k] + crossed[it, k].astype(F32)).astype(BF16)
            rs_copy(it, k, z, col_of(chips[k], 0)).start()

        def cross(k):
            def put(at, value):
                crossing[it, k, at, :] = value.astype(BF16)

            products(col_of(chips[k], 1), put)
            core_copy(it, k).start()

        def keep(k):
            def put(at, value):
                partial[k, at, :] = value

            products(col_of(chips[k], 0), put)

        cross(0)
        cross(1)
        keep(0)
        pass_on(0)
        cross(2)
        keep(1)
        pass_on(1)
        keep(2)
        pass_on(2)
        cross(3)
        keep(3)

    def await_sums(it):
        core_copy(it, 3).wait_recv()
        wait_for(crossing.at[it], core_send.at[it])
        wait_for(outgoing.at[it], rs_send.at[it])
        wait_for(outgoing.at[it], rs_recv.at[it])

    def collect(it, rows):
        summed = partial[3, rows, :] + crossed[it, 3, rows, :].astype(F32)
        for k in range(3):
            summed = summed + incoming[it, lax.rem(z + chips[k], SIDE), rows, :].astype(F32)
        return summed * degree[rows, :]

    def exchange(it, buffer, send_sem, recv_sem, at, axis, peers):
        others = buffer.at[it, pl.ds(0, len(peers))]

        def start():
            for peer in peers:
                pltpu.make_async_remote_copy(
                    src_ref=buffer.at[it, at],
                    dst_ref=buffer.at[it, at],
                    send_sem=send_sem.at[it],
                    recv_sem=recv_sem.at[it],
                    device_id={axis: peer},
                    device_id_type=MESH,
                ).start()

        def finish():
            wait_for(others, recv_sem.at[it])
            wait_for(others, send_sem.at[it])
            total = buffer[it, 0]
            for n in range(1, len(peers) + 1):
                total = total + buffer[it, n]
            return total

        return start, finish

    def gram_of(it):
        along_z = exchange(it, gram_z, gz_send, gz_recv, mine_c, "cols", z_peers)
        along_plane = exchange(it, gram_p, gp_send, gp_recv, mine_r, "rows", plane)

        def first():
            rows = rows_ref[...]
            both = lax.dot_general(
                rows, rows, (((0,), (0,)), ((), ())), precision=HIGHEST, preferred_element_type=F32
            )
            gram = both[:B] + pltpu.roll(both[B:], B, 1)
            gram_z[it, mine_c] = jnp.where(low_h, gram[:H], pltpu.roll(gram[H:], B, 1))
            along_z[0]()

        def second():
            gram_p[it, mine_r] = along_z[1]()
            along_plane[0]()

        def last():
            total = along_plane[1]() * (1.0 / total_rows)
            return jnp.concatenate([total, pltpu.roll(total, B, 1)], axis=0)

        return first, second, last

    for pair in range(4):
        fill_own(0, pair)
    table[NB] = jnp.zeros((B, LANES), BF16)
    pl.semaphore_wait(barrier, len(x_peers) + len(y_peers) + len(z_peers))
    for half in range(2):
        send_own(0, half)

    shares = [(0, 1), (2,), (3, 4), (5, 6, 7)]

    def arranging(n):
        for g in shares[n]:
            arrange(g)

    all_gather(0, arranging)
    multiply(0)

    await_sums(0)
    for half in range(2):
        for pair in (2 * half, 2 * half + 1):
            rows = slice(2 * pair * H, 2 * pair * H + B)
            rows_ref[rows, :] = collect(0, rows)
            fill_own(1, pair)
        send_own(1, half)
    first, second, last = gram_of(0)
    all_gather(1, lambda n: n == 0 and first())
    second()
    multiply(1)
    factor = twice(inverse_factor(last()))
    await_sums(1)
    rows_ref[...] = times_transpose(collect(1, slice(None)), factor)

    first, second, last = gram_of(1)
    first()
    second()
    factor = twice(inverse_factor(last()))
    rows_ref[...] = times_transpose(rows_ref[...], factor)
    for t in range(H):
        out_ref[:, t * LANES : (t + 1) * LANES] = rows_ref[pl.ds(t, R, stride=H), :]


def body(affinity, block_columns, block_counts, inv_degree, panel):
    total_rows = float(affinity.shape[0] * affinity.shape[1] * lax.axis_size("rows") * B)
    dma = pltpu.SemaphoreType.DMA
    out = pl.pallas_call(
        functools.partial(kernel, total_rows),
        out_shape=jax.ShapeDtypeStruct((R, H * LANES), F32),
        in_specs=[
            pl.BlockSpec(memory_space=pltpu.HBM),
        ]
        * 5,
        out_specs=pl.BlockSpec(memory_space=pltpu.VMEM),
        scratch_shapes=[
            pltpu.SMEM((G, R, S), jnp.int32),
            pltpu.SMEM((G, R), jnp.int32),
            pltpu.SMEM((G * R * S,), jnp.int32),
            pltpu.VMEM((R, B), F32),
            pltpu.VMEM((R, H * LANES), F32),
            pltpu.VMEM((G, R, S, H * LANES), BF16),
            pltpu.VMEM((G * R, B, S * B), BF16),
            pltpu.VMEM((S * H, LANES), F32),
            pltpu.VMEM((R * H, LANES), F32),
            pltpu.VMEM((R * H, LANES), F32),
            pltpu.VMEM((R * H, LANES), F32),
            pltpu.VMEM((ITERS, NB // 2, B, LANES), BF16),
            pltpu.VMEM((NB + 1, B, LANES), BF16),
            pltpu.VMEM((ITERS, SIDE, R * H, LANES), BF16),
            pltpu.VMEM((ITERS, SIDE, R * H, LANES), BF16),
            pltpu.VMEM((SIDE, R * H, LANES), F32),
            pltpu.VMEM((ITERS, SIDE - 1, R * H, LANES), BF16),
            pltpu.VMEM((ITERS, SIDE, R * H, LANES), BF16),
            pltpu.VMEM((ITERS, G, H, LANES), F32),
            pltpu.VMEM((ITERS, SIDE * SIDE, H, LANES), F32),
            dma((4,)),
            dma((G,)),
            dma((ITERS,)),
            dma((ITERS, 12)),
            dma((ITERS,)),
            dma((ITERS, SIDE)),
            dma((ITERS,)),
            dma((ITERS,)),
            dma((ITERS,)),
            dma((ITERS,)),
            dma((ITERS,)),
            dma((ITERS,)),
        ],
        compiler_params=pltpu.CompilerParams(
            collective_id=0, has_side_effects=True, vmem_limit_bytes=60 * 1024 * 1024
        ),
        name="subspace",
    )(
        block_columns[:, :, 0],
        block_counts[:, :, 0],
        affinity[:, :, 0],
        inv_degree[0],
        panel[0],
    )
    return out[None]


def solution(mesh):
    return jax.shard_map(
        body,
        mesh=mesh,
        in_specs=(
            P(None, "rows", "cols", None, None),
            P(None, "rows", "cols", None),
            P(None, "rows", "cols"),
            P("cols", "rows", None),
            P("cols", "rows", None),
        ),
        out_specs=P("cols", "rows", None),
        check_vma=False,
    )
```

```python
import functools

import jax
import jax.numpy as jnp
from jax import lax
from jax.experimental import pallas as pl
from jax.experimental.pallas import tpu as pltpu
from jax.sharding import PartitionSpec as P

ITERS = 2
SIDE = 4
B = 64
G = 8
R = 8
S = 8
H = B // 2
LANES = 128
NB = 128
PANEL = 8
DISTANCES = (2, 1, 3)
MESH = pl.DeviceIdType.MESH
HIGHEST = lax.Precision.HIGHEST
F32 = jnp.float32
BF16 = jnp.bfloat16


def low_lanes(rows):
    return lax.broadcasted_iota(jnp.int32, (rows, LANES), 1) < B


def trade(u, v, low):
    crossed = pltpu.roll(jnp.where(low, v, u), B, 1)
    return jnp.where(low, u, crossed), jnp.where(low, crossed, v)


def inverse_factor(gram):
    row = lax.broadcasted_iota(jnp.int32, (B, LANES), 0)
    lane = lax.broadcasted_iota(jnp.int32, (B, LANES), 1)
    m = jnp.where(lane < B, gram, jnp.where(lane - B == row, 1.0, 0.0).astype(F32))
    done = []
    for start in range(0, B, PANEL):
        offset = start % 8
        height = B - start + offset
        rows = lax.broadcasted_iota(jnp.int32, (height, LANES), 0)
        columns = [
            jnp.broadcast_to(m[:, start + j : start + j + 1], (height, LANES)) for j in range(PANEL)
        ]
        for j in range(PANEL):
            at = offset + j
            ratio = columns[j] * (1.0 / columns[j][at : at + 1, :])
            ratio = jnp.where(rows > at, ratio, 0.0)
            for later in range(j + 1, PANEL):
                columns[later] = columns[later] - ratio * columns[later][at : at + 1, :]
            m = m - ratio * m[at : at + 1, :]
        if offset + PANEL == 8:
            done.append(m[:8])
            m = m[8:]
    m = jnp.concatenate(done, axis=0)
    pivots = jnp.sum(jnp.where(lane == row, m, 0.0), axis=1, keepdims=True)
    return m * lax.rsqrt(pivots)


def twice(inverse):
    low = low_lanes(B)
    upper = jnp.where(low, pltpu.roll(inverse, B, 1), 0.0)
    lower = jnp.where(low, 0.0, inverse)
    return jnp.concatenate([upper, lower], axis=0)


def times_transpose(rows, factor):
    return lax.dot_general(
        rows, factor, (((1,), (1,)), ((), ())), precision=HIGHEST, preferred_element_type=F32
    )


def kernel(
    total_rows,
    columns_hbm, counts_hbm, affinity_ref, inverse_hbm, panel_hbm,
    out_ref,
    columns_ref, counts_ref, index_ref, inverse_ref, panel_ref,
    raw, blocks, stage, degree, rows_ref, pack, gathered, table, crossing, crossed, partial,
    outgoing, incoming, gram_z, gram_p,
    in_sem, raw_sem, ag_send, ag_recv, core_send, core_recv, rs_send, rs_recv, gz_send, gz_recv, gp_send, gp_recv,
):
    mine_r, mine_c = lax.axis_index("rows"), lax.axis_index("cols")
    x, y = mine_r // SIDE, lax.rem(mine_r, SIDE)
    z, core = mine_c // 2, lax.rem(mine_c, 2)

    def row_of(dx, dy):
        return lax.rem(x + dx + SIDE, SIDE) * SIDE + lax.rem(y + dy + SIDE, SIDE)

    def col_of(dz, dc):
        return lax.rem(z + dz, SIDE) * 2 + lax.rem(core + dc, 2)

    x_peers = [row_of(d, 0) for d in DISTANCES]
    y_peers = [row_of(0, d) for d in DISTANCES]
    order = [(2, 0), (2, 1), (1, 0), (3, 0), (1, 1), (3, 1), (0, 1)]
    z_peers = [col_of(*d) for d in order]
    plane = [row_of(dx, dy) for dx, dy in ((2, 2), (2, 1), (2, 3), (1, 2), (3, 2), (2, 0), (0, 2))]
    plane += [row_of(dx, dy) for dx in (1, 3) for dy in (1, 3)] + [row_of(*d) for d in ((1, 0), (3, 0), (0, 1), (0, 3))]

    arrivals = [
        pltpu.make_async_copy(source, target, in_sem.at[n])
        for n, (source, target) in enumerate(
            (
                (panel_hbm, panel_ref),
                (inverse_hbm, inverse_ref),
                (columns_hbm, columns_ref),
                (counts_hbm, counts_ref),
            )
        )
    ]
    for arrival in arrivals:
        arrival.start()
    for g in range(G):
        pltpu.make_async_copy(affinity_ref.at[g], raw.at[g], raw_sem.at[g]).start()

    barrier = pltpu.get_barrier_semaphore()
    for peer in x_peers + y_peers:
        pl.semaphore_signal(barrier, inc=1, device_id={"rows": peer}, device_id_type=MESH)
    for peer in z_peers:
        pl.semaphore_signal(barrier, inc=1, device_id={"cols": peer}, device_id_type=MESH)

    for arrival in arrivals:
        arrival.wait()

    spread = lax.broadcasted_iota(jnp.int32, (H, B), 1) // 2 == lax.broadcasted_iota(jnp.int32, (H, B), 0)
    picked = jnp.concatenate(
        [jnp.where(spread, jnp.broadcast_to(inverse_ref[i : i + 1, :], (H, B)), 0.0) for i in range(R)], axis=0
    )
    halves = (
        lax.rem(lax.broadcasted_iota(jnp.int32, (B, LANES), 0), 2)
        == lax.broadcasted_iota(jnp.int32, (B, LANES), 1) // B
    )
    degree[...] = jnp.dot(
        picked, jnp.where(halves, 1.0, 0.0).astype(F32), precision=HIGHEST, preferred_element_type=F32
    )
    for t in range(H):
        rows_ref[pl.ds(t, R, stride=H), :] = panel_ref[:, t * LANES : (t + 1) * LANES]

    low_h = low_lanes(H)
    low_b = low_lanes(B)

    def fill_own(it, pair):
        rows = slice(2 * pair * H, 2 * pair * H + B)
        scaled = rows_ref[rows, :] * degree[rows, :]
        even, odd = trade(scaled[:H], scaled[H:], low_h)
        pack[pl.ds(pair * B, H, stride=2), :] = even
        pack[pl.ds(pair * B + 1, H, stride=2), :] = odd
        gathered[it, mine_r * 4 + pair] = pack[pair * B : (pair + 1) * B, :].astype(BF16)

    def ag_copy(it, slot, group, peer):
        both = pl.ds(2 * slot, 2)
        return pltpu.make_async_remote_copy(
            src_ref=gathered.at[it, both],
            dst_ref=gathered.at[it, both],
            send_sem=ag_send.at[it],
            recv_sem=ag_recv.at[it, group],
            device_id={"rows": peer},
            device_id_type=MESH,
        )

    def wait_for(ref, sem):
        pltpu.make_async_copy(ref, ref, sem).wait()

    def expand(it, slot):
        pair = gathered[it, slot]
        zero = jnp.zeros_like(pair)
        table[2 * slot] = jnp.where(low_b, pair, zero)
        table[2 * slot + 1] = jnp.where(low_b, zero, pair)

    def all_gather(it, meanwhile):
        def slot_of(dx, dy, half):
            return row_of(dx, dy) * 2 + half

        def send(dx, dy, half, stage):
            along_y = (half == 0) == (stage == 1)
            for n, peer in enumerate(y_peers if along_y else x_peers):
                ag_copy(it, slot_of(dx, dy, half), 6 * stage + 3 * half + n, peer).start()

        def unpack(dx, dy, half):
            for pair in range(2):
                expand(it, 2 * slot_of(dx, dy, half) + pair)

        def take(n, half):
            d = -DISTANCES[n]
            at = (d, 0) if half == 0 else (0, d)
            wait_for(gathered.at[it, pl.ds(0, 2)], ag_recv.at[it, 3 * half + n])
            send(*at, half, 1)
            return at

        def take_all(n, half):
            d = -DISTANCES[n]
            wait_for(gathered.at[it, pl.ds(0, 2 * SIDE)], ag_recv.at[it, 6 + 3 * half + n])
            for e in range(SIDE):
                at = (e, d) if half == 0 else (d, e)
                unpack(*at, half)

        send(0, 0, 0, 1)
        send(0, 0, 1, 1)
        for half in range(2):
            unpack(0, 0, half)
        meanwhile(0)
        for n in (1, 2):
            for half in range(2):
                at = take(n, half)
                unpack(*at, half)
        meanwhile(1)
        for half in range(2):
            at = take(0, half)
            unpack(*at, half)
        meanwhile(2)
        for n in (1, 2, 0):
            for half in range(2):
                take_all(n, half)
        meanwhile(3)
        wait_for(gathered.at[it, pl.ds(0, 60)], ag_send.at[it])

    def send_own(it, half):
        for n, peer in enumerate(y_peers if half else x_peers):
            ag_copy(it, mine_r * 2 + half, 3 * half + n, peer).start()

    def arrange(g):
        pltpu.make_async_copy(affinity_ref.at[g], raw.at[g], raw_sem.at[g]).wait()

        def one(i, carry):
            count = counts_ref[g, i]
            for s in range(S):
                index_ref[(g * R + i) * S + s] = jnp.where(s < count, columns_ref[g, i, s], NB)
            for t in range(H):
                stage[pl.ds(t, S, stride=H), :] = raw[g, i, :, t * LANES : (t + 1) * LANES].astype(F32)
            for u in range(S // 2):
                upper, lower = trade(
                    stage[2 * u * H : (2 * u + 1) * H, :], stage[(2 * u + 1) * H : (2 * u + 2) * H, :], low_h
                )
                blocks[g * R + i, 0:H, u * LANES : (u + 1) * LANES] = upper.astype(BF16)
                blocks[g * R + i, H:B, u * LANES : (u + 1) * LANES] = lower.astype(BF16)
            return carry

        lax.fori_loop(0, R, one, 0)

    def gathered_blocks(g, i):
        first = (g * R + i) * S
        return jnp.concatenate([table[index_ref[first + s]] for s in range(S)], axis=0)

    def product(g, i):
        left = jnp.concatenate([blocks[g * R + i], blocks[g * R + i + 1]], axis=0)
        right = jnp.concatenate([gathered_blocks(g, i), gathered_blocks(g, i + 1)], axis=1)
        o = jnp.dot(left, right, preferred_element_type=F32)
        terms = []
        for quarter in (o[:B, :LANES], o[B:, LANES:]):
            even, odd = quarter[:H], quarter[H:]
            terms.append(jnp.where(low_h, even, odd) + pltpu.roll(jnp.where(low_h, odd, even), B, 1))
        return jnp.concatenate(terms, axis=0)

    partner = col_of(0, 1)
    chips = (2, 1, 3, 0)

    def core_copy(it, k):
        return pltpu.make_async_remote_copy(
            src_ref=crossing.at[it, k],
            dst_ref=crossed.at[it, k],
            send_sem=core_send.at[it],
            recv_sem=core_recv.at[it, k],
            device_id={"cols": partner},
            device_id_type=MESH,
        )

    def rs_copy(it, k, slot, peer):
        return pltpu.make_async_remote_copy(
            src_ref=outgoing.at[it, k],
            dst_ref=incoming.at[it, slot],
            send_sem=rs_send.at[it],
            recv_sem=rs_recv.at[it],
            device_id={"cols": peer},
            device_id_type=MESH,
        )

    def products(g, put):
        for i in range(0, R, 2):
            put(slice(i * H, i * H + B), product(g, i))

    def multiply(it):
        def pass_on(k):
            core_copy(it, k).wait_recv()
            outgoing[it, k] = (partial[k] + crossed[it, k].astype(F32)).astype(BF16)
            rs_copy(it, k, z, col_of(chips[k], 0)).start()

        def cross(k):
            def put(at, value):
                crossing[it, k, at, :] = value.astype(BF16)

            products(col_of(chips[k], 1), put)
            core_copy(it, k).start()

        def keep(k):
            def put(at, value):
                partial[k, at, :] = value

            products(col_of(chips[k], 0), put)

        cross(0)
        cross(1)
        keep(0)
        pass_on(0)
        cross(2)
        keep(1)
        pass_on(1)
        keep(2)
        pass_on(2)
        cross(3)
        keep(3)

    def await_sums(it):
        core_copy(it, 3).wait_recv()
        wait_for(crossing.at[it], core_send.at[it])
        wait_for(outgoing.at[it], rs_send.at[it])
        wait_for(outgoing.at[it], rs_recv.at[it])

    def collect(it, rows):
        summed = partial[3, rows, :] + crossed[it, 3, rows, :].astype(F32)
        for k in range(3):
            summed = summed + incoming[it, lax.rem(z + chips[k], SIDE), rows, :].astype(F32)
        return summed * degree[rows, :]

    def exchange(it, buffer, send_sem, recv_sem, at, axis, peers):
        others = buffer.at[it, pl.ds(0, len(peers))]

        def start():
            for peer in peers:
                pltpu.make_async_remote_copy(
                    src_ref=buffer.at[it, at],
                    dst_ref=buffer.at[it, at],
                    send_sem=send_sem.at[it],
                    recv_sem=recv_sem.at[it],
                    device_id={axis: peer},
                    device_id_type=MESH,
                ).start()

        def finish():
            wait_for(others, recv_sem.at[it])
            wait_for(others, send_sem.at[it])
            total = buffer[it, 0]
            for n in range(1, len(peers) + 1):
                total = total + buffer[it, n]
            return total

        return start, finish

    def gram_of(it):
        along_z = exchange(it, gram_z, gz_send, gz_recv, mine_c, "cols", z_peers)
        along_plane = exchange(it, gram_p, gp_send, gp_recv, mine_r, "rows", plane)

        def first():
            rows = rows_ref[...]
            both = lax.dot_general(
                rows, rows, (((0,), (0,)), ((), ())), precision=HIGHEST, preferred_element_type=F32
            )
            gram = both[:B] + pltpu.roll(both[B:], B, 1)
            gram_z[it, mine_c] = jnp.where(low_h, gram[:H], pltpu.roll(gram[H:], B, 1))
            along_z[0]()

        def second():
            gram_p[it, mine_r] = along_z[1]()
            along_plane[0]()

        def last():
            total = along_plane[1]() * (1.0 / total_rows)
            return jnp.concatenate([total, pltpu.roll(total, B, 1)], axis=0)

        return first, second, last

    for pair in range(4):
        fill_own(0, pair)
    table[NB] = jnp.zeros((B, LANES), BF16)
    pl.semaphore_wait(barrier, len(x_peers) + len(y_peers) + len(z_peers))
    for half in range(2):
        send_own(0, half)

    shares = [(0, 1), (2,), (3, 4), (5, 6, 7)]

    def arranging(n):
        for g in shares[n]:
            arrange(g)

    all_gather(0, arranging)
    multiply(0)

    await_sums(0)
    for half in range(2):
        for pair in (2 * half, 2 * half + 1):
            rows = slice(2 * pair * H, 2 * pair * H + B)
            rows_ref[rows, :] = collect(0, rows)
            fill_own(1, pair)
        send_own(1, half)
    first, second, last = gram_of(0)
    reducing = {0: first, 3: second}
    all_gather(1, lambda n: n in reducing and reducing[n]())
    multiply(1)
    factor = twice(inverse_factor(last()))
    await_sums(1)
    rows_ref[...] = times_transpose(collect(1, slice(None)), factor)

    first, second, last = gram_of(1)
    first()
    second()
    factor = twice(inverse_factor(last()))
    rows_ref[...] = times_transpose(rows_ref[...], factor)
    for t in range(H):
        out_ref[:, t * LANES : (t + 1) * LANES] = rows_ref[pl.ds(t, R, stride=H), :]


def body(affinity, block_columns, block_counts, inv_degree, panel):
    total_rows = float(affinity.shape[0] * affinity.shape[1] * lax.axis_size("rows") * B)
    dma = pltpu.SemaphoreType.DMA
    out = pl.pallas_call(
        functools.partial(kernel, total_rows),
        out_shape=jax.ShapeDtypeStruct((R, H * LANES), F32),
        in_specs=[
            pl.BlockSpec(memory_space=pltpu.HBM),
        ]
        * 5,
        out_specs=pl.BlockSpec(memory_space=pltpu.VMEM),
        scratch_shapes=[
            pltpu.SMEM((G, R, S), jnp.int32),
            pltpu.SMEM((G, R), jnp.int32),
            pltpu.SMEM((G * R * S,), jnp.int32),
            pltpu.VMEM((R, B), F32),
            pltpu.VMEM((R, H * LANES), F32),
            pltpu.VMEM((G, R, S, H * LANES), BF16),
            pltpu.VMEM((G * R, B, S * B), BF16),
            pltpu.VMEM((S * H, LANES), F32),
            pltpu.VMEM((R * H, LANES), F32),
            pltpu.VMEM((R * H, LANES), F32),
            pltpu.VMEM((R * H, LANES), F32),
            pltpu.VMEM((ITERS, NB // 2, B, LANES), BF16),
            pltpu.VMEM((NB + 1, B, LANES), BF16),
            pltpu.VMEM((ITERS, SIDE, R * H, LANES), BF16),
            pltpu.VMEM((ITERS, SIDE, R * H, LANES), BF16),
            pltpu.VMEM((SIDE, R * H, LANES), F32),
            pltpu.VMEM((ITERS, SIDE - 1, R * H, LANES), BF16),
            pltpu.VMEM((ITERS, SIDE, R * H, LANES), BF16),
            pltpu.VMEM((ITERS, G, H, LANES), F32),
            pltpu.VMEM((ITERS, SIDE * SIDE, H, LANES), F32),
            dma((4,)),
            dma((G,)),
            dma((ITERS,)),
            dma((ITERS, 12)),
            dma((ITERS,)),
            dma((ITERS, SIDE)),
            dma((ITERS,)),
            dma((ITERS,)),
            dma((ITERS,)),
            dma((ITERS,)),
            dma((ITERS,)),
            dma((ITERS,)),
        ],
        compiler_params=pltpu.CompilerParams(
            collective_id=0, has_side_effects=True, vmem_limit_bytes=40 * 1024 * 1024
        ),
        name="subspace",
    )(
        *(
            pltpu.with_memory_space_constraint(argument, pltpu.HBM)
            for argument in (block_columns[:, :, 0], block_counts[:, :, 0], affinity[:, :, 0], inv_degree[0], panel[0])
        )
    )
    return out[None]


def solution(mesh):
    return jax.shard_map(
        body,
        mesh=mesh,
        in_specs=(
            P(None, "rows", "cols", None, None),
            P(None, "rows", "cols", None),
            P(None, "rows", "cols"),
            P("cols", "rows", None),
            P("cols", "rows", None),
        ),
        out_specs=P("cols", "rows", None),
        check_vma=False,
    )
```

```python
import functools

import jax
import jax.numpy as jnp
from jax import lax
from jax.experimental import pallas as pl
from jax.experimental.pallas import tpu as pltpu
from jax.sharding import PartitionSpec as P

ITERS = 2
SIDE = 4
B = 64
G = 8
R = 8
S = 8
H = B // 2
LANES = 128
NB = 128
PANEL = 8
DISTANCES = (2, 1, 3)
MESH = pl.DeviceIdType.MESH
HIGHEST = lax.Precision.HIGHEST
F32 = jnp.float32
BF16 = jnp.bfloat16


def low_lanes(rows):
    return lax.broadcasted_iota(jnp.int32, (rows, LANES), 1) < B


def trade(u, v, low):
    crossed = pltpu.roll(jnp.where(low, v, u), B, 1)
    return jnp.where(low, u, crossed), jnp.where(low, crossed, v)


def inverse_factor(gram):
    row = lax.broadcasted_iota(jnp.int32, (B, LANES), 0)
    lane = lax.broadcasted_iota(jnp.int32, (B, LANES), 1)
    m = jnp.where(lane < B, gram, jnp.where(lane - B == row, 1.0, 0.0).astype(F32))
    done = []
    for start in range(0, B, PANEL):
        offset = start % 8
        height = B - start + offset
        rows = lax.broadcasted_iota(jnp.int32, (height, LANES), 0)
        columns = [
            jnp.broadcast_to(m[:, start + j : start + j + 1], (height, LANES)) for j in range(PANEL)
        ]
        for j in range(PANEL):
            at = offset + j
            ratio = columns[j] * (1.0 / columns[j][at : at + 1, :])
            ratio = jnp.where(rows > at, ratio, 0.0)
            for later in range(j + 1, PANEL):
                columns[later] = columns[later] - ratio * columns[later][at : at + 1, :]
            m = m - ratio * m[at : at + 1, :]
        if offset + PANEL == 8:
            done.append(m[:8])
            m = m[8:]
    m = jnp.concatenate(done, axis=0)
    pivots = jnp.sum(jnp.where(lane == row, m, 0.0), axis=1, keepdims=True)
    return m * lax.rsqrt(pivots)


def twice(inverse):
    low = low_lanes(B)
    upper = jnp.where(low, pltpu.roll(inverse, B, 1), 0.0)
    lower = jnp.where(low, 0.0, inverse)
    return jnp.concatenate([upper, lower], axis=0)


def times_transpose(rows, factor):
    return lax.dot_general(
        rows, factor, (((1,), (1,)), ((), ())), precision=HIGHEST, preferred_element_type=F32
    )


def kernel(
    total_rows,
    columns_hbm, counts_hbm, affinity_ref, inverse_hbm, panel_hbm,
    out_ref,
    columns_ref, counts_ref, index_ref, inverse_ref, panel_ref,
    raw, blocks, stage, degree, rows_ref, pack, gathered, table, crossing, crossed, partial,
    outgoing, incoming, gram_z, gram_p,
    in_sem, raw_sem, ag_send, ag_recv, core_send, core_recv, rs_send, rs_recv, gz_send, gz_recv, gp_send, gp_recv,
):
    mine_r, mine_c = lax.axis_index("rows"), lax.axis_index("cols")
    x, y = mine_r // SIDE, lax.rem(mine_r, SIDE)
    z, core = mine_c // 2, lax.rem(mine_c, 2)

    def row_of(dx, dy):
        return lax.rem(x + dx + SIDE, SIDE) * SIDE + lax.rem(y + dy + SIDE, SIDE)

    def col_of(dz, dc):
        return lax.rem(z + dz, SIDE) * 2 + lax.rem(core + dc, 2)

    x_peers = [row_of(d, 0) for d in DISTANCES]
    y_peers = [row_of(0, d) for d in DISTANCES]
    order = [(2, 0), (2, 1), (1, 0), (3, 0), (1, 1), (3, 1), (0, 1)]
    z_peers = [col_of(*d) for d in order]
    plane = [row_of(dx, dy) for dx, dy in ((2, 2), (2, 1), (2, 3), (1, 2), (3, 2), (2, 0), (0, 2))]
    plane += [row_of(dx, dy) for dx in (1, 3) for dy in (1, 3)] + [row_of(*d) for d in ((1, 0), (3, 0), (0, 1), (0, 3))]

    arrivals = [
        pltpu.make_async_copy(source, target, in_sem.at[n])
        for n, (source, target) in enumerate(
            (
                (panel_hbm, panel_ref),
                (inverse_hbm, inverse_ref),
                (columns_hbm, columns_ref),
                (counts_hbm, counts_ref),
            )
        )
    ]
    for arrival in arrivals:
        arrival.start()
    for g in range(G):
        pltpu.make_async_copy(affinity_ref.at[g], raw.at[g], raw_sem.at[g]).start()

    barrier = pltpu.get_barrier_semaphore()
    for peer in x_peers + y_peers:
        pl.semaphore_signal(barrier, inc=1, device_id={"rows": peer}, device_id_type=MESH)
    for peer in z_peers:
        pl.semaphore_signal(barrier, inc=1, device_id={"cols": peer}, device_id_type=MESH)

    for arrival in arrivals:
        arrival.wait()

    spread = lax.broadcasted_iota(jnp.int32, (H, B), 1) // 2 == lax.broadcasted_iota(jnp.int32, (H, B), 0)
    picked = jnp.concatenate(
        [jnp.where(spread, jnp.broadcast_to(inverse_ref[i : i + 1, :], (H, B)), 0.0) for i in range(R)], axis=0
    )
    halves = (
        lax.rem(lax.broadcasted_iota(jnp.int32, (B, LANES), 0), 2)
        == lax.broadcasted_iota(jnp.int32, (B, LANES), 1) // B
    )
    degree[...] = jnp.dot(
        picked, jnp.where(halves, 1.0, 0.0).astype(F32), precision=HIGHEST, preferred_element_type=F32
    )
    for t in range(H):
        rows_ref[pl.ds(t, R, stride=H), :] = panel_ref[:, t * LANES : (t + 1) * LANES]

    low_h = low_lanes(H)
    low_b = low_lanes(B)

    def fill_own(it, pair):
        rows = slice(2 * pair * H, 2 * pair * H + B)
        scaled = rows_ref[rows, :] * degree[rows, :]
        even, odd = trade(scaled[:H], scaled[H:], low_h)
        pack[pl.ds(pair * B, H, stride=2), :] = even
        pack[pl.ds(pair * B + 1, H, stride=2), :] = odd
        gathered[it, mine_r * 4 + pair] = pack[pair * B : (pair + 1) * B, :].astype(BF16)

    def ag_copy(it, slot, group, peer):
        both = pl.ds(2 * slot, 2)
        return pltpu.make_async_remote_copy(
            src_ref=gathered.at[it, both],
            dst_ref=gathered.at[it, both],
            send_sem=ag_send.at[it],
            recv_sem=ag_recv.at[it, group],
            device_id={"rows": peer},
            device_id_type=MESH,
        )

    def wait_for(ref, sem):
        pltpu.make_async_copy(ref, ref, sem).wait()

    def expand(it, slot):
        pair = gathered[it, slot]
        zero = jnp.zeros_like(pair)
        table[2 * slot] = jnp.where(low_b, pair, zero)
        table[2 * slot + 1] = jnp.where(low_b, zero, pair)

    def all_gather(it, meanwhile):
        def slot_of(dx, dy, half):
            return row_of(dx, dy) * 2 + half

        def send(dx, dy, half, stage):
            along_y = (half == 0) == (stage == 1)
            for n, peer in enumerate(y_peers if along_y else x_peers):
                ag_copy(it, slot_of(dx, dy, half), 6 * stage + 3 * half + n, peer).start()

        def unpack(dx, dy, half):
            for pair in range(2):
                expand(it, 2 * slot_of(dx, dy, half) + pair)

        def take(n, half):
            d = -DISTANCES[n]
            at = (d, 0) if half == 0 else (0, d)
            wait_for(gathered.at[it, pl.ds(0, 2)], ag_recv.at[it, 3 * half + n])
            send(*at, half, 1)
            return at

        def take_all(n, half):
            d = -DISTANCES[n]
            wait_for(gathered.at[it, pl.ds(0, 2 * SIDE)], ag_recv.at[it, 6 + 3 * half + n])
            for e in range(SIDE):
                at = (e, d) if half == 0 else (d, e)
                unpack(*at, half)

        send(0, 0, 0, 1)
        send(0, 0, 1, 1)
        for half in range(2):
            unpack(0, 0, half)
        meanwhile(0)
        for n in (1, 2):
            for half in range(2):
                at = take(n, half)
                unpack(*at, half)
        meanwhile(1)
        for half in range(2):
            at = take(0, half)
            unpack(*at, half)
        meanwhile(2)
        for n in (1, 2, 0):
            for half in range(2):
                take_all(n, half)
        meanwhile(3)
        wait_for(gathered.at[it, pl.ds(0, 60)], ag_send.at[it])

    def send_own(it, half):
        for n, peer in enumerate(y_peers if half else x_peers):
            ag_copy(it, mine_r * 2 + half, 3 * half + n, peer).start()

    def arrange(g):
        pltpu.make_async_copy(affinity_ref.at[g], raw.at[g], raw_sem.at[g]).wait()

        def one(i, carry):
            count = counts_ref[g, i]
            for s in range(S):
                index_ref[(g * R + i) * S + s] = jnp.where(s < count, columns_ref[g, i, s], NB)
            for t in range(H):
                stage[t * S : (t + 1) * S, :] = raw[g, i, :, t * LANES : (t + 1) * LANES].astype(F32)
            for u in range(S // 2):
                upper, lower = trade(
                    stage[pl.ds(2 * u, H, stride=S), :], stage[pl.ds(2 * u + 1, H, stride=S), :], low_h
                )
                blocks[g * R + i, 0:H, u * LANES : (u + 1) * LANES] = upper.astype(BF16)
                blocks[g * R + i, H:B, u * LANES : (u + 1) * LANES] = lower.astype(BF16)
            return carry

        lax.fori_loop(0, R, one, 0)

    def gathered_blocks(g, i):
        first = (g * R + i) * S
        return jnp.concatenate([table[index_ref[first + s]] for s in range(S)], axis=0)

    def product(g, i):
        left = jnp.concatenate([blocks[g * R + i], blocks[g * R + i + 1]], axis=0)
        right = jnp.concatenate([gathered_blocks(g, i), gathered_blocks(g, i + 1)], axis=1)
        o = jnp.dot(left, right, preferred_element_type=F32)
        terms = []
        for quarter in (o[:B, :LANES], o[B:, LANES:]):
            even, odd = quarter[:H], quarter[H:]
            terms.append(jnp.where(low_h, even, odd) + pltpu.roll(jnp.where(low_h, odd, even), B, 1))
        return jnp.concatenate(terms, axis=0)

    partner = col_of(0, 1)
    chips = (2, 1, 3, 0)

    def half_rows(half):
        return slice(half * R * H // 2, (half + 1) * R * H // 2)

    def core_copy(it, k, half):
        rows = pl.ds(half * R * H // 2, R * H // 2)
        return pltpu.make_async_remote_copy(
            src_ref=crossing.at[it, k, rows],
            dst_ref=crossed.at[it, k, rows],
            send_sem=core_send.at[it],
            recv_sem=core_recv.at[it, SIDE * half + k],
            device_id={"cols": partner},
            device_id_type=MESH,
        )

    def rs_copy(it, k, half, peer):
        rows = pl.ds(half * R * H // 2, R * H // 2)
        return pltpu.make_async_remote_copy(
            src_ref=outgoing.at[it, k, rows],
            dst_ref=incoming.at[it, z, rows],
            send_sem=rs_send.at[it],
            recv_sem=rs_recv.at[it, half],
            device_id={"cols": peer},
            device_id_type=MESH,
        )

    def products(g, half, put):
        for i in range(half * R // 2, (half + 1) * R // 2, 2):
            put(slice(i * H, i * H + B), product(g, i))

    def multiply(it):
        def cross(k, half):
            def put(at, value):
                crossing[it, k, at, :] = value.astype(BF16)

            products(col_of(chips[k], 1), half, put)

        def keep(k, half):
            def put(at, value):
                partial[k, at, :] = value

            products(col_of(chips[k], 0), half, put)

        def pass_on(k, half):
            core_copy(it, k, half).wait_recv()
            rows = half_rows(half)
            outgoing[it, k, rows, :] = (partial[k, rows, :] + crossed[it, k, rows, :].astype(F32)).astype(BF16)
            rs_copy(it, k, half, col_of(chips[k], 0)).start()

        for half in range(2):
            cross(0, half)
            cross(1, half)
            core_copy(it, 0, half).start()
            core_copy(it, 1, half).start()
            if half == 1:
                pass_on(2, 0)
            cross(2, half)
            keep(0, half)
            core_copy(it, 2, half).start()
            keep(1, half)
            keep(2, half)
            pass_on(0, half)
            pass_on(1, half)
        cross(3, 0)
        cross(3, 1)
        core_copy(it, 3, 0).start()
        core_copy(it, 3, 1).start()
        pass_on(2, 1)
        keep(3, 0)
        keep(3, 1)

    def await_sums(it, half):
        core_copy(it, 3, half).wait_recv()
        wait_for(gathered.at[it, pl.ds(0, 6)], rs_recv.at[it, half])
        if half == 1:
            wait_for(crossing.at[it], core_send.at[it])
            wait_for(outgoing.at[it], rs_send.at[it])

    def collect(it, rows):
        summed = partial[3, rows, :] + crossed[it, 3, rows, :].astype(F32)
        for k in range(3):
            summed = summed + incoming[it, lax.rem(z + chips[k], SIDE), rows, :].astype(F32)
        return summed * degree[rows, :]

    def exchange(it, buffer, send_sem, recv_sem, at, axis, peers):
        others = buffer.at[it, pl.ds(0, len(peers))]

        def start():
            for peer in peers:
                pltpu.make_async_remote_copy(
                    src_ref=buffer.at[it, at],
                    dst_ref=buffer.at[it, at],
                    send_sem=send_sem.at[it],
                    recv_sem=recv_sem.at[it],
                    device_id={axis: peer},
                    device_id_type=MESH,
                ).start()

        def finish():
            wait_for(others, recv_sem.at[it])
            wait_for(others, send_sem.at[it])
            total = buffer[it, 0]
            for n in range(1, len(peers) + 1):
                total = total + buffer[it, n]
            return total

        return start, finish

    def gram_of(it):
        along_z = exchange(it, gram_z, gz_send, gz_recv, mine_c, "cols", z_peers)
        along_plane = exchange(it, gram_p, gp_send, gp_recv, mine_r, "rows", plane)

        def first():
            rows = rows_ref[...]
            both = lax.dot_general(
                rows, rows, (((0,), (0,)), ((), ())), precision=HIGHEST, preferred_element_type=F32
            )
            gram = both[:B] + pltpu.roll(both[B:], B, 1)
            gram_z[it, mine_c] = jnp.where(low_h, gram[:H], pltpu.roll(gram[H:], B, 1))
            along_z[0]()

        def second():
            gram_p[it, mine_r] = along_z[1]()
            along_plane[0]()

        def last():
            total = along_plane[1]() * (1.0 / total_rows)
            return jnp.concatenate([total, pltpu.roll(total, B, 1)], axis=0)

        return first, second, last

    for pair in range(4):
        fill_own(0, pair)
    table[NB] = jnp.zeros((B, LANES), BF16)
    pl.semaphore_wait(barrier, len(x_peers) + len(y_peers) + len(z_peers))
    for half in range(2):
        send_own(0, half)

    shares = [(0, 1), (2,), (3, 4), (5, 6, 7)]

    def arranging(n):
        for g in shares[n]:
            arrange(g)

    all_gather(0, arranging)
    multiply(0)

    for half in range(2):
        await_sums(0, half)
        for pair in (2 * half, 2 * half + 1):
            rows = slice(2 * pair * H, 2 * pair * H + B)
            rows_ref[rows, :] = collect(0, rows)
            fill_own(1, pair)
        send_own(1, half)
    first, second, last = gram_of(0)
    reducing = {0: first, 3: second}
    all_gather(1, lambda n: n in reducing and reducing[n]())
    multiply(1)
    factor = twice(inverse_factor(last()))
    for half in range(2):
        await_sums(1, half)
    rows_ref[...] = times_transpose(collect(1, slice(None)), factor)

    first, second, last = gram_of(1)
    first()
    second()
    factor = twice(inverse_factor(last()))
    rows_ref[...] = times_transpose(rows_ref[...], factor)
    for t in range(H):
        out_ref[:, t * LANES : (t + 1) * LANES] = rows_ref[pl.ds(t, R, stride=H), :]


def body(affinity, block_columns, block_counts, inv_degree, panel):
    total_rows = float(affinity.shape[0] * affinity.shape[1] * lax.axis_size("rows") * B)
    dma = pltpu.SemaphoreType.DMA
    out = pl.pallas_call(
        functools.partial(kernel, total_rows),
        out_shape=jax.ShapeDtypeStruct((R, H * LANES), F32),
        in_specs=[
            pl.BlockSpec(memory_space=pltpu.HBM),
        ]
        * 5,
        out_specs=pl.BlockSpec(memory_space=pltpu.VMEM),
        scratch_shapes=[
            pltpu.SMEM((G, R, S), jnp.int32),
            pltpu.SMEM((G, R), jnp.int32),
            pltpu.SMEM((G * R * S,), jnp.int32),
            pltpu.VMEM((R, B), F32),
            pltpu.VMEM((R, H * LANES), F32),
            pltpu.VMEM((G, R, S, H * LANES), BF16),
            pltpu.VMEM((G * R, B, S * B), BF16),
            pltpu.VMEM((S * H, LANES), F32),
            pltpu.VMEM((R * H, LANES), F32),
            pltpu.VMEM((R * H, LANES), F32),
            pltpu.VMEM((R * H, LANES), F32),
            pltpu.VMEM((ITERS, NB // 2, B, LANES), BF16),
            pltpu.VMEM((NB + 1, B, LANES), BF16),
            pltpu.VMEM((ITERS, SIDE, R * H, LANES), BF16),
            pltpu.VMEM((ITERS, SIDE, R * H, LANES), BF16),
            pltpu.VMEM((SIDE, R * H, LANES), F32),
            pltpu.VMEM((ITERS, SIDE - 1, R * H, LANES), BF16),
            pltpu.VMEM((ITERS, SIDE, R * H, LANES), BF16),
            pltpu.VMEM((ITERS, G, H, LANES), F32),
            pltpu.VMEM((ITERS, SIDE * SIDE, H, LANES), F32),
            dma((4,)),
            dma((G,)),
            dma((ITERS,)),
            dma((ITERS, 12)),
            dma((ITERS,)),
            dma((ITERS, 2 * SIDE)),
            dma((ITERS,)),
            dma((ITERS, 2)),
            dma((ITERS,)),
            dma((ITERS,)),
            dma((ITERS,)),
            dma((ITERS,)),
        ],
        compiler_params=pltpu.CompilerParams(
            collective_id=0, has_side_effects=True, vmem_limit_bytes=40 * 1024 * 1024
        ),
        name="subspace",
    )(
        *(
            pltpu.with_memory_space_constraint(argument, pltpu.HBM)
            for argument in (block_columns[:, :, 0], block_counts[:, :, 0], affinity[:, :, 0], inv_degree[0], panel[0])
        )
    )
    return out[None]


def solution(mesh):
    return jax.shard_map(
        body,
        mesh=mesh,
        in_specs=(
            P(None, "rows", "cols", None, None),
            P(None, "rows", "cols", None),
            P(None, "rows", "cols"),
            P("cols", "rows", None),
            P("cols", "rows", None),
        ),
        out_specs=P("cols", "rows", None),
        check_vma=False,
    )
```

```python
import functools

import jax
import jax.numpy as jnp
from jax import lax
from jax.experimental import pallas as pl
from jax.experimental.pallas import tpu as pltpu
from jax.sharding import PartitionSpec as P

ITERS = 2
SIDE = 4
B = 64
G = 8
R = 8
S = 8
H = B // 2
LANES = 128
NB = 128
PANEL = 8
DISTANCES = (2, 1, 3)
MESH = pl.DeviceIdType.MESH
HIGHEST = lax.Precision.HIGHEST
F32 = jnp.float32
BF16 = jnp.bfloat16


def low_lanes(rows):
    return lax.broadcasted_iota(jnp.int32, (rows, LANES), 1) < B


def trade(u, v, low):
    crossed = pltpu.roll(jnp.where(low, v, u), B, 1)
    return jnp.where(low, u, crossed), jnp.where(low, crossed, v)


def inverse_factor(gram):
    row = lax.broadcasted_iota(jnp.int32, (B, LANES), 0)
    lane = lax.broadcasted_iota(jnp.int32, (B, LANES), 1)
    m = jnp.where(lane < B, gram, jnp.where(lane - B == row, 1.0, 0.0).astype(F32))
    done = []
    for start in range(0, B, PANEL):
        offset = start % 8
        height = B - start + offset
        rows = lax.broadcasted_iota(jnp.int32, (height, LANES), 0)
        columns = [
            jnp.broadcast_to(m[:, start + j : start + j + 1], (height, LANES)) for j in range(PANEL)
        ]
        for j in range(PANEL):
            at = offset + j
            ratio = columns[j] * (1.0 / columns[j][at : at + 1, :])
            ratio = jnp.where(rows > at, ratio, 0.0)
            for later in range(j + 1, PANEL):
                columns[later] = columns[later] - ratio * columns[later][at : at + 1, :]
            m = m - ratio * m[at : at + 1, :]
        if offset + PANEL == 8:
            done.append(m[:8])
            m = m[8:]
    m = jnp.concatenate(done, axis=0)
    pivots = jnp.sum(jnp.where(lane == row, m, 0.0), axis=1, keepdims=True)
    return m * lax.rsqrt(pivots)


def twice(inverse):
    low = low_lanes(B)
    upper = jnp.where(low, pltpu.roll(inverse, B, 1), 0.0)
    lower = jnp.where(low, 0.0, inverse)
    return jnp.concatenate([upper, lower], axis=0)


def times_transpose(rows, factor):
    return lax.dot_general(
        rows, factor, (((1,), (1,)), ((), ())), precision=HIGHEST, preferred_element_type=F32
    )


def kernel(
    total_rows,
    columns_hbm, counts_hbm, affinity_ref, inverse_hbm, panel_hbm,
    out_ref,
    columns_ref, counts_ref, index_ref, inverse_ref, panel_ref,
    raw, blocks, stage, degree, rows_ref, pack, gathered, table, crossing, crossed, partial,
    outgoing, incoming, gram_z, gram_p,
    in_sem, raw_sem, ag_send, ag_recv, core_send, core_recv, rs_send, rs_recv, gz_send, gz_recv, gp_send, gp_recv,
):
    mine_r, mine_c = lax.axis_index("rows"), lax.axis_index("cols")
    x, y = mine_r // SIDE, lax.rem(mine_r, SIDE)
    z, core = mine_c // 2, lax.rem(mine_c, 2)

    def row_of(dx, dy):
        return lax.rem(x + dx + SIDE, SIDE) * SIDE + lax.rem(y + dy + SIDE, SIDE)

    def col_of(dz, dc):
        return lax.rem(z + dz, SIDE) * 2 + lax.rem(core + dc, 2)

    x_peers = [row_of(d, 0) for d in DISTANCES]
    y_peers = [row_of(0, d) for d in DISTANCES]
    order = [(2, 0), (2, 1), (1, 0), (3, 0), (1, 1), (3, 1), (0, 1)]
    z_peers = [col_of(*d) for d in order]
    plane = [row_of(dx, dy) for dx, dy in ((2, 2), (2, 1), (2, 3), (1, 2), (3, 2), (2, 0), (0, 2))]
    plane += [row_of(dx, dy) for dx in (1, 3) for dy in (1, 3)] + [row_of(*d) for d in ((1, 0), (3, 0), (0, 1), (0, 3))]

    arrivals = [
        pltpu.make_async_copy(source, target, in_sem.at[n])
        for n, (source, target) in enumerate(
            (
                (panel_hbm, panel_ref),
                (inverse_hbm, inverse_ref),
                (columns_hbm, columns_ref),
                (counts_hbm, counts_ref),
            )
        )
    ]
    for arrival in arrivals:
        arrival.start()
    for g in range(G):
        pltpu.make_async_copy(affinity_ref.at[g], raw.at[g], raw_sem.at[g]).start()

    barrier = pltpu.get_barrier_semaphore()
    for peer in x_peers + y_peers:
        pl.semaphore_signal(barrier, inc=1, device_id={"rows": peer}, device_id_type=MESH)
    for peer in z_peers:
        pl.semaphore_signal(barrier, inc=1, device_id={"cols": peer}, device_id_type=MESH)

    for arrival in arrivals:
        arrival.wait()

    spread = lax.broadcasted_iota(jnp.int32, (H, B), 1) // 2 == lax.broadcasted_iota(jnp.int32, (H, B), 0)
    picked = jnp.concatenate(
        [jnp.where(spread, jnp.broadcast_to(inverse_ref[i : i + 1, :], (H, B)), 0.0) for i in range(R)], axis=0
    )
    halves = (
        lax.rem(lax.broadcasted_iota(jnp.int32, (B, LANES), 0), 2)
        == lax.broadcasted_iota(jnp.int32, (B, LANES), 1) // B
    )
    degree[...] = jnp.dot(
        picked, jnp.where(halves, 1.0, 0.0).astype(F32), precision=HIGHEST, preferred_element_type=F32
    )
    for t in range(H):
        rows_ref[pl.ds(t, R, stride=H), :] = panel_ref[:, t * LANES : (t + 1) * LANES]

    low_h = low_lanes(H)
    low_b = low_lanes(B)

    def fill_own(it, pair):
        rows = slice(2 * pair * H, 2 * pair * H + B)
        scaled = rows_ref[rows, :] * degree[rows, :]
        even, odd = trade(scaled[:H], scaled[H:], low_h)
        pack[pl.ds(pair * B, H, stride=2), :] = even
        pack[pl.ds(pair * B + 1, H, stride=2), :] = odd
        gathered[it, mine_r * 4 + pair] = pack[pair * B : (pair + 1) * B, :].astype(BF16)

    def ag_copy(it, slot, group, peer):
        both = pl.ds(2 * slot, 2)
        return pltpu.make_async_remote_copy(
            src_ref=gathered.at[it, both],
            dst_ref=gathered.at[it, both],
            send_sem=ag_send.at[it],
            recv_sem=ag_recv.at[it, group],
            device_id={"rows": peer},
            device_id_type=MESH,
        )

    def wait_for(ref, sem):
        pltpu.make_async_copy(ref, ref, sem).wait()

    def expand(it, slot):
        pair = gathered[it, slot]
        zero = jnp.zeros_like(pair)
        table[2 * slot] = jnp.where(low_b, pair, zero)
        table[2 * slot + 1] = jnp.where(low_b, zero, pair)

    def all_gather(it, meanwhile):
        def slot_of(dx, dy, half):
            return row_of(dx, dy) * 2 + half

        def send(dx, dy, half, stage):
            along_y = (half == 0) == (stage == 1)
            for n, peer in enumerate(y_peers if along_y else x_peers):
                ag_copy(it, slot_of(dx, dy, half), 6 * stage + 3 * half + n, peer).start()

        def unpack(dx, dy, half):
            for pair in range(2):
                expand(it, 2 * slot_of(dx, dy, half) + pair)

        def take(n, half):
            d = -DISTANCES[n]
            at = (d, 0) if half == 0 else (0, d)
            wait_for(gathered.at[it, pl.ds(0, 2)], ag_recv.at[it, 3 * half + n])
            send(*at, half, 1)
            return at

        def take_all(n, half):
            d = -DISTANCES[n]
            wait_for(gathered.at[it, pl.ds(0, 2 * SIDE)], ag_recv.at[it, 6 + 3 * half + n])
            for e in range(SIDE):
                at = (e, d) if half == 0 else (d, e)
                unpack(*at, half)

        send(0, 0, 0, 1)
        send(0, 0, 1, 1)
        for half in range(2):
            unpack(0, 0, half)
        meanwhile(0)
        for n in (1, 2):
            for half in range(2):
                at = take(n, half)
                unpack(*at, half)
        meanwhile(1)
        for half in range(2):
            at = take(0, half)
            unpack(*at, half)
        meanwhile(2)
        for n in (1, 2, 0):
            for half in range(2):
                take_all(n, half)
        meanwhile(3)
        wait_for(gathered.at[it, pl.ds(0, 60)], ag_send.at[it])

    def send_own(it, half):
        for n, peer in enumerate(y_peers if half else x_peers):
            ag_copy(it, mine_r * 2 + half, 3 * half + n, peer).start()

    def arrange(g):
        pltpu.make_async_copy(affinity_ref.at[g], raw.at[g], raw_sem.at[g]).wait()

        def one(i, carry):
            count = counts_ref[g, i]
            for s in range(S):
                index_ref[(g * R + i) * S + s] = jnp.where(s < count, columns_ref[g, i, s], NB)
            for t in range(H):
                stage[t * S : (t + 1) * S, :] = raw[g, i, :, t * LANES : (t + 1) * LANES].astype(F32)
            for u in range(S // 2):
                upper, lower = trade(
                    stage[pl.ds(2 * u, H, stride=S), :], stage[pl.ds(2 * u + 1, H, stride=S), :], low_h
                )
                blocks[g * R + i, 0:H, u * LANES : (u + 1) * LANES] = upper.astype(BF16)
                blocks[g * R + i, H:B, u * LANES : (u + 1) * LANES] = lower.astype(BF16)
            return carry

        lax.fori_loop(0, R, one, 0)

    def gathered_blocks(g, i):
        first = (g * R + i) * S
        return jnp.concatenate([table[index_ref[first + s]] for s in range(S)], axis=0)

    def product(g, i):
        left = jnp.concatenate([blocks[g * R + i], blocks[g * R + i + 1]], axis=0)
        right = jnp.concatenate([gathered_blocks(g, i), gathered_blocks(g, i + 1)], axis=1)
        o = jnp.dot(left, right, preferred_element_type=F32)
        terms = []
        for quarter in (o[:B, :LANES], o[B:, LANES:]):
            even, odd = quarter[:H], quarter[H:]
            terms.append(jnp.where(low_h, even, odd) + pltpu.roll(jnp.where(low_h, odd, even), B, 1))
        return jnp.concatenate(terms, axis=0)

    partner = col_of(0, 1)
    chips = (2, 1, 3, 0)

    def half_rows(half):
        return slice(half * R * H // 2, (half + 1) * R * H // 2)

    def core_copy(it, k, half):
        rows = pl.ds(half * R * H // 2, R * H // 2)
        return pltpu.make_async_remote_copy(
            src_ref=crossing.at[it, k, rows],
            dst_ref=crossed.at[it, k, rows],
            send_sem=core_send.at[it],
            recv_sem=core_recv.at[it, SIDE * half + k],
            device_id={"cols": partner},
            device_id_type=MESH,
        )

    def rs_copy(it, k, half, peer):
        rows = pl.ds(half * R * H // 2, R * H // 2)
        return pltpu.make_async_remote_copy(
            src_ref=outgoing.at[it, k, rows],
            dst_ref=incoming.at[it, z, rows],
            send_sem=rs_send.at[it],
            recv_sem=rs_recv.at[it, half],
            device_id={"cols": peer},
            device_id_type=MESH,
        )

    def products(g, half, put):
        for i in range(half * R // 2, (half + 1) * R // 2, 2):
            put(slice(i * H, i * H + B), product(g, i))

    def multiply(it):
        def cross(k, half):
            def put(at, value):
                crossing[it, k, at, :] = value.astype(BF16)

            products(col_of(chips[k], 1), half, put)

        def keep(k, half):
            def put(at, value):
                partial[k, at, :] = value

            products(col_of(chips[k], 0), half, put)

        def pass_on(k, half):
            core_copy(it, k, half).wait_recv()
            rows = half_rows(half)
            outgoing[it, k, rows, :] = (partial[k, rows, :] + crossed[it, k, rows, :].astype(F32)).astype(BF16)
            rs_copy(it, k, half, col_of(chips[k], 0)).start()

        for half in range(2):
            cross(0, half)
            cross(1, half)
            core_copy(it, 0, half).start()
            core_copy(it, 1, half).start()
            if half == 1:
                pass_on(2, 0)
            cross(2, half)
            keep(0, half)
            core_copy(it, 2, half).start()
            keep(1, half)
            keep(2, half)
            pass_on(0, half)
            pass_on(1, half)
        cross(3, 0)
        cross(3, 1)
        core_copy(it, 3, 0).start()
        core_copy(it, 3, 1).start()
        pass_on(2, 1)
        keep(3, 0)
        keep(3, 1)

    def await_sums(it, half):
        core_copy(it, 3, half).wait_recv()
        wait_for(gathered.at[it, pl.ds(0, 6)], rs_recv.at[it, half])
        if half == 1:
            wait_for(crossing.at[it], core_send.at[it])
            wait_for(outgoing.at[it], rs_send.at[it])

    def collect(it, rows):
        summed = partial[3, rows, :] + crossed[it, 3, rows, :].astype(F32)
        for k in range(3):
            summed = summed + incoming[it, lax.rem(z + chips[k], SIDE), rows, :].astype(F32)
        return summed * degree[rows, :]

    def exchange(it, buffer, send_sem, recv_sem, at, axis, peers):
        others = buffer.at[it, pl.ds(0, len(peers))]

        def start():
            for peer in peers:
                pltpu.make_async_remote_copy(
                    src_ref=buffer.at[it, at],
                    dst_ref=buffer.at[it, at],
                    send_sem=send_sem.at[it],
                    recv_sem=recv_sem.at[it],
                    device_id={axis: peer},
                    device_id_type=MESH,
                ).start()

        def finish():
            wait_for(others, recv_sem.at[it])
            wait_for(others, send_sem.at[it])
            total = buffer[it, 0]
            for n in range(1, len(peers) + 1):
                total = total + buffer[it, n]
            return total

        return start, finish

    def gram_of(it):
        along_z = exchange(it, gram_z, gz_send, gz_recv, mine_c, "cols", z_peers)
        along_plane = exchange(it, gram_p, gp_send, gp_recv, mine_r, "rows", plane)

        def first():
            rows = rows_ref[...]
            both = lax.dot_general(
                rows, rows, (((0,), (0,)), ((), ())), precision=HIGHEST, preferred_element_type=F32
            )
            gram = both[:B] + pltpu.roll(both[B:], B, 1)
            gram_z[it, mine_c] = jnp.where(low_h, gram[:H], pltpu.roll(gram[H:], B, 1))
            along_z[0]()

        def second():
            gram_p[it, mine_r] = along_z[1]()
            along_plane[0]()

        def last():
            total = along_plane[1]() * (1.0 / total_rows)
            return jnp.concatenate([total, pltpu.roll(total, B, 1)], axis=0)

        return first, second, last

    for pair in range(4):
        fill_own(0, pair)
    table[NB] = jnp.zeros((B, LANES), BF16)
    pl.semaphore_wait(barrier, len(x_peers) + len(y_peers) + len(z_peers))
    for half in range(2):
        send_own(0, half)

    shares = [(0, 1, 2), (3,), (4, 5, 6, 7), ()]

    def arranging(n):
        for g in shares[n]:
            arrange(g)

    all_gather(0, arranging)
    multiply(0)

    for half in range(2):
        await_sums(0, half)
        for pair in (2 * half, 2 * half + 1):
            rows = slice(2 * pair * H, 2 * pair * H + B)
            rows_ref[rows, :] = collect(0, rows)
            fill_own(1, pair)
        send_own(1, half)
    first, second, last = gram_of(0)
    reducing = {0: first, 3: second}
    all_gather(1, lambda n: n in reducing and reducing[n]())
    multiply(1)
    factor = twice(inverse_factor(last()))
    for half in range(2):
        await_sums(1, half)
    rows_ref[...] = times_transpose(collect(1, slice(None)), factor)

    first, second, last = gram_of(1)
    first()
    second()
    factor = twice(inverse_factor(last()))
    rows_ref[...] = times_transpose(rows_ref[...], factor)
    for t in range(H):
        out_ref[:, t * LANES : (t + 1) * LANES] = rows_ref[pl.ds(t, R, stride=H), :]


def body(affinity, block_columns, block_counts, inv_degree, panel):
    total_rows = float(affinity.shape[0] * affinity.shape[1] * lax.axis_size("rows") * B)
    dma = pltpu.SemaphoreType.DMA
    out = pl.pallas_call(
        functools.partial(kernel, total_rows),
        out_shape=jax.ShapeDtypeStruct((R, H * LANES), F32),
        in_specs=[
            pl.BlockSpec(memory_space=pltpu.HBM),
        ]
        * 5,
        out_specs=pl.BlockSpec(memory_space=pltpu.VMEM),
        scratch_shapes=[
            pltpu.SMEM((G, R, S), jnp.int32),
            pltpu.SMEM((G, R), jnp.int32),
            pltpu.SMEM((G * R * S,), jnp.int32),
            pltpu.VMEM((R, B), F32),
            pltpu.VMEM((R, H * LANES), F32),
            pltpu.VMEM((G, R, S, H * LANES), BF16),
            pltpu.VMEM((G * R, B, S * B), BF16),
            pltpu.VMEM((S * H, LANES), F32),
            pltpu.VMEM((R * H, LANES), F32),
            pltpu.VMEM((R * H, LANES), F32),
            pltpu.VMEM((R * H, LANES), F32),
            pltpu.VMEM((ITERS, NB // 2, B, LANES), BF16),
            pltpu.VMEM((NB + 1, B, LANES), BF16),
            pltpu.VMEM((ITERS, SIDE, R * H, LANES), BF16),
            pltpu.VMEM((ITERS, SIDE, R * H, LANES), BF16),
            pltpu.VMEM((SIDE, R * H, LANES), F32),
            pltpu.VMEM((ITERS, SIDE - 1, R * H, LANES), BF16),
            pltpu.VMEM((ITERS, SIDE, R * H, LANES), BF16),
            pltpu.VMEM((ITERS, G, H, LANES), F32),
            pltpu.VMEM((ITERS, SIDE * SIDE, H, LANES), F32),
            dma((4,)),
            dma((G,)),
            dma((ITERS,)),
            dma((ITERS, 12)),
            dma((ITERS,)),
            dma((ITERS, 2 * SIDE)),
            dma((ITERS,)),
            dma((ITERS, 2)),
            dma((ITERS,)),
            dma((ITERS,)),
            dma((ITERS,)),
            dma((ITERS,)),
        ],
        compiler_params=pltpu.CompilerParams(
            collective_id=0, has_side_effects=True, vmem_limit_bytes=40 * 1024 * 1024
        ),
        name="subspace",
    )(
        *(
            pltpu.with_memory_space_constraint(argument, pltpu.HBM)
            for argument in (block_columns[:, :, 0], block_counts[:, :, 0], affinity[:, :, 0], inv_degree[0], panel[0])
        )
    )
    return out[None]


def solution(mesh):
    return jax.shard_map(
        body,
        mesh=mesh,
        in_specs=(
            P(None, "rows", "cols", None, None),
            P(None, "rows", "cols", None),
            P(None, "rows", "cols"),
            P("cols", "rows", None),
            P("cols", "rows", None),
        ),
        out_specs=P("cols", "rows", None),
        check_vma=False,
    )
```

```python
import functools

import jax
import jax.numpy as jnp
from jax import lax
from jax.experimental import pallas as pl
from jax.experimental.pallas import tpu as pltpu
from jax.sharding import PartitionSpec as P

ITERS = 2
SIDE = 4
B = 64
G = 8
R = 8
S = 8
H = B // 2
LANES = 128
NB = 128
PANEL = 8
DISTANCES = (2, 1, 3)
MESH = pl.DeviceIdType.MESH
HIGHEST = lax.Precision.HIGHEST
F32 = jnp.float32
BF16 = jnp.bfloat16


def low_lanes(rows):
    return lax.broadcasted_iota(jnp.int32, (rows, LANES), 1) < B


def trade(u, v, low):
    crossed = pltpu.roll(jnp.where(low, v, u), B, 1)
    return jnp.where(low, u, crossed), jnp.where(low, crossed, v)


def inverse_factor(gram):
    row = lax.broadcasted_iota(jnp.int32, (B, LANES), 0)
    lane = lax.broadcasted_iota(jnp.int32, (B, LANES), 1)
    m = jnp.where(lane < B, gram, jnp.where(lane - B == row, 1.0, 0.0).astype(F32))
    done = []
    for start in range(0, B, PANEL):
        offset = start % 8
        height = B - start + offset
        rows = lax.broadcasted_iota(jnp.int32, (height, LANES), 0)
        columns = [
            jnp.broadcast_to(m[:, start + j : start + j + 1], (height, LANES)) for j in range(PANEL)
        ]
        for j in range(PANEL):
            at = offset + j
            ratio = columns[j] * (1.0 / columns[j][at : at + 1, :])
            ratio = jnp.where(rows > at, ratio, 0.0)
            for later in range(j + 1, PANEL):
                columns[later] = columns[later] - ratio * columns[later][at : at + 1, :]
            m = m - ratio * m[at : at + 1, :]
        if offset + PANEL == 8:
            done.append(m[:8])
            m = m[8:]
    m = jnp.concatenate(done, axis=0)
    pivots = jnp.sum(jnp.where(lane == row, m, 0.0), axis=1, keepdims=True)
    return m * lax.rsqrt(pivots)


def twice(inverse):
    low = low_lanes(B)
    upper = jnp.where(low, pltpu.roll(inverse, B, 1), 0.0)
    lower = jnp.where(low, 0.0, inverse)
    return jnp.concatenate([upper, lower], axis=0)


def times_transpose(rows, factor):
    return lax.dot_general(
        rows, factor, (((1,), (1,)), ((), ())), precision=HIGHEST, preferred_element_type=F32
    )


def kernel(
    total_rows,
    columns_hbm, counts_hbm, affinity_ref, inverse_hbm, panel_hbm,
    out_ref,
    columns_ref, counts_ref, index_ref, inverse_ref, panel_ref,
    raw, blocks, stage, degree, rows_ref, pack, gathered, table, crossing, crossed, partial,
    outgoing, incoming, gram_z, gram_p,
    in_sem, raw_sem, ag_send, ag_recv, core_send, core_recv, rs_send, rs_recv, gz_send, gz_recv, gp_send, gp_recv,
):
    mine_r, mine_c = lax.axis_index("rows"), lax.axis_index("cols")
    x, y = mine_r // SIDE, lax.rem(mine_r, SIDE)
    z, core = mine_c // 2, lax.rem(mine_c, 2)

    def row_of(dx, dy):
        return lax.rem(x + dx + SIDE, SIDE) * SIDE + lax.rem(y + dy + SIDE, SIDE)

    def col_of(dz, dc):
        return lax.rem(z + dz, SIDE) * 2 + lax.rem(core + dc, 2)

    x_peers = [row_of(d, 0) for d in DISTANCES]
    y_peers = [row_of(0, d) for d in DISTANCES]
    order = [(2, 0), (2, 1), (1, 0), (3, 0), (1, 1), (3, 1), (0, 1)]
    z_peers = [col_of(*d) for d in order]
    plane = [row_of(dx, dy) for dx, dy in ((2, 2), (2, 1), (2, 3), (1, 2), (3, 2), (2, 0), (0, 2))]
    plane += [row_of(dx, dy) for dx in (1, 3) for dy in (1, 3)] + [row_of(*d) for d in ((1, 0), (3, 0), (0, 1), (0, 3))]

    arrivals = [
        pltpu.make_async_copy(source, target, in_sem.at[n])
        for n, (source, target) in enumerate(
            (
                (panel_hbm, panel_ref),
                (inverse_hbm, inverse_ref),
                (columns_hbm, columns_ref),
                (counts_hbm, counts_ref),
            )
        )
    ]
    for arrival in arrivals:
        arrival.start()
    for g in range(G):
        pltpu.make_async_copy(affinity_ref.at[g], raw.at[g], raw_sem.at[g]).start()

    barrier = pltpu.get_barrier_semaphore()
    for peer in x_peers + y_peers:
        pl.semaphore_signal(barrier, inc=1, device_id={"rows": peer}, device_id_type=MESH)
    for peer in z_peers:
        pl.semaphore_signal(barrier, inc=1, device_id={"cols": peer}, device_id_type=MESH)

    for arrival in arrivals:
        arrival.wait()

    spread = lax.broadcasted_iota(jnp.int32, (H, B), 1) // 2 == lax.broadcasted_iota(jnp.int32, (H, B), 0)
    picked = jnp.concatenate(
        [jnp.where(spread, jnp.broadcast_to(inverse_ref[i : i + 1, :], (H, B)), 0.0) for i in range(R)], axis=0
    )
    halves = (
        lax.rem(lax.broadcasted_iota(jnp.int32, (B, LANES), 0), 2)
        == lax.broadcasted_iota(jnp.int32, (B, LANES), 1) // B
    )
    degree[...] = jnp.dot(
        picked, jnp.where(halves, 1.0, 0.0).astype(F32), precision=HIGHEST, preferred_element_type=F32
    )
    for t in range(H):
        rows_ref[pl.ds(t, R, stride=H), :] = panel_ref[:, t * LANES : (t + 1) * LANES]

    low_h = low_lanes(H)
    low_b = low_lanes(B)

    def fill_own(it, pair):
        rows = slice(2 * pair * H, 2 * pair * H + B)
        scaled = rows_ref[rows, :] * degree[rows, :]
        even, odd = trade(scaled[:H], scaled[H:], low_h)
        pack[pl.ds(pair * B, H, stride=2), :] = even
        pack[pl.ds(pair * B + 1, H, stride=2), :] = odd
        gathered[it, mine_r * 4 + pair] = pack[pair * B : (pair + 1) * B, :].astype(BF16)

    def ag_copy(it, slot, group, peer):
        both = pl.ds(2 * slot, 2)
        return pltpu.make_async_remote_copy(
            src_ref=gathered.at[it, both],
            dst_ref=gathered.at[it, both],
            send_sem=ag_send.at[it],
            recv_sem=ag_recv.at[it, group],
            device_id={"rows": peer},
            device_id_type=MESH,
        )

    def wait_for(ref, sem):
        pltpu.make_async_copy(ref, ref, sem).wait()

    def expand(it, slot):
        pair = gathered[it, slot]
        zero = jnp.zeros_like(pair)
        table[2 * slot] = jnp.where(low_b, pair, zero)
        table[2 * slot + 1] = jnp.where(low_b, zero, pair)

    def all_gather(it, meanwhile):
        def slot_of(dx, dy, half):
            return row_of(dx, dy) * 2 + half

        def send(dx, dy, half, stage):
            along_y = (half == 0) == (stage == 1)
            for n, peer in enumerate(y_peers if along_y else x_peers):
                ag_copy(it, slot_of(dx, dy, half), 6 * stage + 3 * half + n, peer).start()

        def unpack(dx, dy, half):
            for pair in range(2):
                expand(it, 2 * slot_of(dx, dy, half) + pair)

        def take(n, half):
            d = -DISTANCES[n]
            at = (d, 0) if half == 0 else (0, d)
            wait_for(gathered.at[it, pl.ds(0, 2)], ag_recv.at[it, 3 * half + n])
            send(*at, half, 1)
            return at

        def take_all(n, half):
            d = -DISTANCES[n]
            wait_for(gathered.at[it, pl.ds(0, 2 * SIDE)], ag_recv.at[it, 6 + 3 * half + n])
            for e in range(SIDE):
                at = (e, d) if half == 0 else (d, e)
                unpack(*at, half)

        send(0, 0, 0, 1)
        send(0, 0, 1, 1)
        for half in range(2):
            unpack(0, 0, half)
        meanwhile(0)
        for n in (1, 2):
            for half in range(2):
                at = take(n, half)
                unpack(*at, half)
        meanwhile(1)
        for half in range(2):
            at = take(0, half)
            unpack(*at, half)
        meanwhile(2)
        for n in (1, 2, 0):
            for half in range(2):
                take_all(n, half)
        meanwhile(3)
        wait_for(gathered.at[it, pl.ds(0, 60)], ag_send.at[it])

    def send_own(it, half):
        for n, peer in enumerate(y_peers if half else x_peers):
            ag_copy(it, mine_r * 2 + half, 3 * half + n, peer).start()

    def arrange(g):
        pltpu.make_async_copy(affinity_ref.at[g], raw.at[g], raw_sem.at[g]).wait()

        def one(i, carry):
            count = counts_ref[g, i]
            for s in range(S):
                index_ref[(g * R + i) * S + s] = jnp.where(s < count, columns_ref[g, i, s], NB)
            for t in range(H):
                stage[t * S : (t + 1) * S, :] = raw[g, i, :, t * LANES : (t + 1) * LANES].astype(F32)
            for u in range(S // 2):
                upper, lower = trade(
                    stage[pl.ds(2 * u, H, stride=S), :], stage[pl.ds(2 * u + 1, H, stride=S), :], low_h
                )
                blocks[g * R + i, 0:H, u * LANES : (u + 1) * LANES] = upper.astype(BF16)
                blocks[g * R + i, H:B, u * LANES : (u + 1) * LANES] = lower.astype(BF16)
            return carry

        lax.fori_loop(0, R, one, 0)

    def gathered_blocks(g, i):
        first = (g * R + i) * S
        return jnp.concatenate([table[index_ref[first + s]] for s in range(S)], axis=0)

    def product(g, i):
        left = jnp.concatenate([blocks[g * R + i], blocks[g * R + i + 1]], axis=0)
        right = jnp.concatenate([gathered_blocks(g, i), gathered_blocks(g, i + 1)], axis=1)
        o = jnp.dot(left, right, preferred_element_type=F32)
        terms = []
        for quarter in (o[:B, :LANES], o[B:, LANES:]):
            even, odd = quarter[:H], quarter[H:]
            terms.append(jnp.where(low_h, even, odd) + pltpu.roll(jnp.where(low_h, odd, even), B, 1))
        return jnp.concatenate(terms, axis=0)

    partner = col_of(0, 1)
    chips = (2, 1, 3, 0)

    def half_rows(half):
        return slice(half * R * H // 2, (half + 1) * R * H // 2)

    def core_copy(it, k, half):
        rows = pl.ds(half * R * H // 2, R * H // 2)
        return pltpu.make_async_remote_copy(
            src_ref=crossing.at[it, k, rows],
            dst_ref=crossed.at[it, k, rows],
            send_sem=core_send.at[it],
            recv_sem=core_recv.at[it, SIDE * half + k],
            device_id={"cols": partner},
            device_id_type=MESH,
        )

    def rs_copy(it, k, half, peer):
        rows = pl.ds(half * R * H // 2, R * H // 2)
        return pltpu.make_async_remote_copy(
            src_ref=outgoing.at[it, k, rows],
            dst_ref=incoming.at[it, z, rows],
            send_sem=rs_send.at[it],
            recv_sem=rs_recv.at[it, half],
            device_id={"cols": peer},
            device_id_type=MESH,
        )

    def products(g, half, put):
        for i in range(half * R // 2, (half + 1) * R // 2, 2):
            put(slice(i * H, i * H + B), product(g, i))

    def multiply(it):
        def cross(k, half):
            def put(at, value):
                crossing[it, k, at, :] = value.astype(BF16)

            products(col_of(chips[k], 1), half, put)

        def keep(k, half):
            def put(at, value):
                partial[k, at, :] = value

            products(col_of(chips[k], 0), half, put)

        def pass_on(k, half):
            core_copy(it, k, half).wait_recv()
            rows = half_rows(half)
            outgoing[it, k, rows, :] = (partial[k, rows, :] + crossed[it, k, rows, :].astype(F32)).astype(BF16)
            rs_copy(it, k, half, col_of(chips[k], 0)).start()

        for half in range(2):
            cross(0, half)
            cross(1, half)
            core_copy(it, 0, half).start()
            core_copy(it, 1, half).start()
            if half == 1:
                pass_on(2, 0)
            cross(2, half)
            keep(0, half)
            core_copy(it, 2, half).start()
            keep(1, half)
            keep(2, half)
            pass_on(0, half)
            pass_on(1, half)
        cross(3, 0)
        cross(3, 1)
        core_copy(it, 3, 0).start()
        core_copy(it, 3, 1).start()
        pass_on(2, 1)
        keep(3, 0)
        keep(3, 1)

    def await_sums(it, half):
        core_copy(it, 3, half).wait_recv()
        wait_for(gathered.at[it, pl.ds(0, 6)], rs_recv.at[it, half])
        if half == 1:
            wait_for(crossing.at[it], core_send.at[it])
            wait_for(outgoing.at[it], rs_send.at[it])

    def collect(it, rows):
        summed = partial[3, rows, :] + crossed[it, 3, rows, :].astype(F32)
        for k in range(3):
            summed = summed + incoming[it, lax.rem(z + chips[k], SIDE), rows, :].astype(F32)
        return summed * degree[rows, :]

    def exchange(it, buffer, send_sem, recv_sem, at, axis, peers):
        others = buffer.at[it, pl.ds(0, len(peers))]

        def start():
            for peer in peers:
                pltpu.make_async_remote_copy(
                    src_ref=buffer.at[it, at],
                    dst_ref=buffer.at[it, at],
                    send_sem=send_sem.at[it],
                    recv_sem=recv_sem.at[it],
                    device_id={axis: peer},
                    device_id_type=MESH,
                ).start()

        def finish():
            wait_for(others, recv_sem.at[it])
            wait_for(others, send_sem.at[it])
            total = buffer[it, 0]
            for n in range(1, len(peers) + 1):
                total = total + buffer[it, n]
            return total

        return start, finish

    def gram_of(it):
        along_z = exchange(it, gram_z, gz_send, gz_recv, mine_c, "cols", z_peers)
        along_plane = exchange(it, gram_p, gp_send, gp_recv, mine_r, "rows", plane)

        def first():
            rows = rows_ref[...]
            both = lax.dot_general(
                rows, rows, (((0,), (0,)), ((), ())), precision=HIGHEST, preferred_element_type=F32
            )
            gram = both[:B] + pltpu.roll(both[B:], B, 1)
            gram_z[it, mine_c] = jnp.where(low_h, gram[:H], pltpu.roll(gram[H:], B, 1))
            along_z[0]()

        def second():
            gram_p[it, mine_r] = along_z[1]()
            along_plane[0]()

        def last():
            total = along_plane[1]() * (1.0 / total_rows)
            return jnp.concatenate([total, pltpu.roll(total, B, 1)], axis=0)

        return first, second, last

    for pair in range(4):
        fill_own(0, pair)
    table[NB] = jnp.zeros((B, LANES), BF16)
    pl.semaphore_wait(barrier, len(x_peers) + len(y_peers) + len(z_peers))
    for half in range(2):
        send_own(0, half)

    shares = [(0, 1), (2, 3), (4, 5, 6, 7), ()]

    def arranging(n):
        for g in shares[n]:
            arrange(g)

    all_gather(0, arranging)
    multiply(0)

    for half in range(2):
        await_sums(0, half)
        for pair in (2 * half, 2 * half + 1):
            rows = slice(2 * pair * H, 2 * pair * H + B)
            rows_ref[rows, :] = collect(0, rows)
            fill_own(1, pair)
        send_own(1, half)
    first, second, last = gram_of(0)
    reducing = {0: first, 3: second}
    all_gather(1, lambda n: n in reducing and reducing[n]())
    multiply(1)
    factor = twice(inverse_factor(last()))
    for half in range(2):
        await_sums(1, half)
    rows_ref[...] = times_transpose(collect(1, slice(None)), factor)

    first, second, last = gram_of(1)
    first()
    second()
    factor = twice(inverse_factor(last()))
    rows_ref[...] = times_transpose(rows_ref[...], factor)
    for t in range(H):
        out_ref[:, t * LANES : (t + 1) * LANES] = rows_ref[pl.ds(t, R, stride=H), :]


def body(affinity, block_columns, block_counts, inv_degree, panel):
    total_rows = float(affinity.shape[0] * affinity.shape[1] * lax.axis_size("rows") * B)
    dma = pltpu.SemaphoreType.DMA
    out = pl.pallas_call(
        functools.partial(kernel, total_rows),
        out_shape=jax.ShapeDtypeStruct((R, H * LANES), F32),
        in_specs=[
            pl.BlockSpec(memory_space=pltpu.HBM),
        ]
        * 5,
        out_specs=pl.BlockSpec(memory_space=pltpu.VMEM),
        scratch_shapes=[
            pltpu.SMEM((G, R, S), jnp.int32),
            pltpu.SMEM((G, R), jnp.int32),
            pltpu.SMEM((G * R * S,), jnp.int32),
            pltpu.VMEM((R, B), F32),
            pltpu.VMEM((R, H * LANES), F32),
            pltpu.VMEM((G, R, S, H * LANES), BF16),
            pltpu.VMEM((G * R, B, S * B), BF16),
            pltpu.VMEM((S * H, LANES), F32),
            pltpu.VMEM((R * H, LANES), F32),
            pltpu.VMEM((R * H, LANES), F32),
            pltpu.VMEM((R * H, LANES), F32),
            pltpu.VMEM((ITERS, NB // 2, B, LANES), BF16),
            pltpu.VMEM((NB + 1, B, LANES), BF16),
            pltpu.VMEM((ITERS, SIDE, R * H, LANES), BF16),
            pltpu.VMEM((ITERS, SIDE, R * H, LANES), BF16),
            pltpu.VMEM((SIDE, R * H, LANES), F32),
            pltpu.VMEM((ITERS, SIDE - 1, R * H, LANES), BF16),
            pltpu.VMEM((ITERS, SIDE, R * H, LANES), BF16),
            pltpu.VMEM((ITERS, G, H, LANES), F32),
            pltpu.VMEM((ITERS, SIDE * SIDE, H, LANES), F32),
            dma((4,)),
            dma((G,)),
            dma((ITERS,)),
            dma((ITERS, 12)),
            dma((ITERS,)),
            dma((ITERS, 2 * SIDE)),
            dma((ITERS,)),
            dma((ITERS, 2)),
            dma((ITERS,)),
            dma((ITERS,)),
            dma((ITERS,)),
            dma((ITERS,)),
        ],
        compiler_params=pltpu.CompilerParams(
            collective_id=0, has_side_effects=True, vmem_limit_bytes=40 * 1024 * 1024
        ),
        name="subspace",
    )(
        *(
            pltpu.with_memory_space_constraint(argument, pltpu.HBM)
            for argument in (block_columns[:, :, 0], block_counts[:, :, 0], affinity[:, :, 0], inv_degree[0], panel[0])
        )
    )
    return out[None]


def solution(mesh):
    return jax.shard_map(
        body,
        mesh=mesh,
        in_specs=(
            P(None, "rows", "cols", None, None),
            P(None, "rows", "cols", None),
            P(None, "rows", "cols"),
            P("cols", "rows", None),
            P("cols", "rows", None),
        ),
        out_specs=P("cols", "rows", None),
        check_vma=False,
    )
```
